32 devices in a mesh: lat: 4 (over y, x), lon: 8 (over z, core).
Axes of the slice: x: 2, y: 2, z: 4, core: 2. Of those that a mesh axis runs over, the one named last changes fastest.
Arguments:
- increment: float32 [4, 20, 128, 512], P(None, None, 'lon', 'lat'), may hold values from -6 to 6
- obs_dep: float32 [4, 20, 128, 512], P(None, None, 'lon', 'lat'), may hold values from -6 to 6
- obs_weight: float32 [4, 20, 128, 512], P(None, None, 'lon', 'lat'), may hold values from 0.1 to 10
- dep_lon: int32 [20, 128, 512], P(None, 'lon', 'lat'), may hold values from -5 to 5
- dep_lat: int32 [20, 128, 512], P(None, 'lon', 'lat'), may hold values from -5 to 5
- frac_lon: float32 [20, 128, 512], P(None, 'lon', 'lat'), may hold values from 0 to 1
- frac_lat: float32 [20, 128, 512], P(None, 'lon', 'lat'), may hold values from 0 to 1
- coupling: float32 [4, 19, 128, 512], P(None, None, 'lon', 'lat'), may hold values from 0.05 to 5
Outputs:
- tl_out: float32 [4, 20, 128, 512], P(None, None, 'lon', 'lat')
- gradient: float32 [4, 20, 128, 512], P(None, None, 'lon', 'lat')
The draws below stay inside these ranges and needn't reach their ends.
All inputs are finite; a program needn't handle non-finite values.
Results may differ from the reference program's by a relative error of at most 0.0003.
Values sent between devices are 32-bit elements; how exact they have to be, the bound alone decides.
A program may use at most 128 MiB of HBM per device.

```python
import math
import jax
import jax.numpy as jnp
from jax import lax

F = 4
LEV = 20
HALO = 6
NLON = 128
NLAT = 512


def touch_ends(array, own_key, least, top_value):
    extent = array.shape
    index_at = [jax.random.randint(jax.random.fold_in(own_key, axis), (), 0, extent[axis]) for axis in range(len(extent))]
    array = array.at[tuple(index_at)].set(least)
    longest = extent.index(max(extent))
    index_at[longest] = (index_at[longest] + 1) % extent[longest]
    return array.at[tuple(index_at)].set(top_value)


def block_levels(rng, dims, cuts, least, top_value):
    def one(dim, blocks):
        heights = jax.random.uniform(jax.random.fold_in(jax.random.fold_in(rng, 6), dim), (blocks,), jnp.float32, least / len(cuts), top_value / len(cuts))
        return jnp.repeat(jnp.exp(heights), dims[dim] // blocks).reshape((-1,) + (1,) * (len(dims) - dim - 1))

    loudness = one(*cuts[0])
    for cut in cuts[1:]:
        loudness = loudness * one(*cut)
    return loudness


def scatter_about(key, dims, width, limit, cuts=(), held_as=jnp.bfloat16):
    gain = block_levels(key, dims, cuts, -0.22, 0.18) if cuts else 1.0
    values = jax.random.normal(key, dims, jnp.float32) * width * gain
    return jnp.minimum(jnp.maximum(values, -limit), limit).astype(held_as)


def setup_inputs(seed: int = 0) -> dict:
    splits = jax.random.split(jax.random.key(seed), 9)
    increment = scatter_about(splits[0], (F, LEV, NLON, NLAT), 1.0, 6.0, ((2, 8), (3, 4)), jnp.float32)
    obs_dep = scatter_about(splits[1], (F, LEV, NLON, NLAT), 1.0, 6.0, ((2, 8), (3, 4)), jnp.float32)
    obs_weight = jnp.clip(jnp.exp(math.log(10.0) - 4.6051702 * jax.random.uniform(splits[2], (F, LEV, NLON, NLAT), jnp.float32) ** block_levels(splits[2], (F, LEV, NLON, NLAT), ((2, 8), (3, 4)), -0.2, 0.2)), 0.1, 10.0)
    dep_lon = touch_ends(jax.random.randint(splits[3], (LEV, NLON, NLAT), 1 - HALO, HALO), jax.random.fold_in(splits[3], 1), 1 - HALO, HALO - 1).astype(jnp.int32)
    dep_lat = touch_ends(jax.random.randint(splits[4], (LEV, NLON, NLAT), 1 - HALO, HALO), jax.random.fold_in(splits[4], 1), 1 - HALO, HALO - 1).astype(jnp.int32)
    frac_lon = jnp.clip(1.0 * jax.random.uniform(splits[5], (LEV, NLON, NLAT), jnp.float32) ** block_levels(splits[5], (LEV, NLON, NLAT), ((1, 8), (2, 4)), -0.2, 0.2), 0.0, 1.0)
    frac_lat = jnp.clip(1.0 * jax.random.uniform(splits[6], (LEV, NLON, NLAT), jnp.float32) ** block_levels(splits[6], (LEV, NLON, NLAT), ((1, 8), (2, 4)), -0.2, 0.2), 0.0, 1.0)
    coupling = jnp.clip(jnp.exp(math.log(5.0) - 4.6051702 * jax.random.uniform(splits[7], (F, LEV - 1, NLON, NLAT), jnp.float32) ** block_levels(splits[7], (F, LEV - 1, NLON, NLAT), ((2, 8), (3, 4)), -0.2, 0.2)), 0.05, 5.0)
    return {"increment": increment, "obs_dep": obs_dep, "obs_weight": obs_weight, "dep_lon": dep_lon, "dep_lat": dep_lat, "frac_lon": frac_lon, "frac_lat": frac_lat, "coupling": coupling}


def column_solve(rhs, coup):
    levels = rhs.shape[1]
    nothing = jnp.zeros_like(rhs[:, 0])
    ratios = []
    primes = []
    for level in range(levels):
        below = coup[:, level - 1] if level > 0 else nothing
        above = coup[:, level] if level < levels - 1 else nothing
        diagonal = 1.0 + below + above
        if level == 0:
            denom = diagonal
            prime = rhs[:, 0] / denom
        else:
            denom = diagonal - below * ratios[-1]
            prime = (rhs[:, level] + below * primes[-1]) / denom
        ratios.append(above / denom)
        primes.append(prime)
    result = [primes[-1]]
    for level in range(levels - 2, -1, -1):
        result.append(primes[level] + ratios[level] * result[-1])
    ordered = result[::-1]
    return jnp.stack(ordered, axis=1)


def level_pairs(olon, olat, flon, flat):
    lon_index = lax.broadcasted_iota(jnp.int32, (NLON, NLAT), 0)
    lat_index = lax.broadcasted_iota(jnp.int32, (NLON, NLAT), 1)
    pairs = []
    for lon_step in (0, 1):
        weight_lon = 1.0 - flon if lon_step == 0 else flon
        for lat_step in (0, 1):
            weight_lat = 1.0 - flat if lat_step == 0 else flat
            lon_src = jnp.mod(lon_index - olon - lon_step, NLON)
            lat_src = lat_index - olat - lat_step
            inside = (lat_src >= 0) & (lat_src < NLAT)
            target = (lon_src * NLAT + jnp.clip(lat_src, 0, NLAT - 1)).astype(jnp.int32)
            weight = jnp.where(inside, weight_lon * weight_lat, jnp.zeros_like(flon))
            pairs.append((target.reshape(-1), weight.reshape(-1)))
    return pairs


def forward_level(args):
    field, olon, olat, flon, flat = args
    fields = field.shape[0]
    flat_src = field.reshape(fields, -1)
    terms = [weight[None] * flat_src[:, target] for target, weight in level_pairs(olon, olat, flon, flat)]
    summed = terms[0] + terms[1] + terms[2] + terms[3]
    return summed.reshape(fields, NLON, NLAT)


def backward_level(args):
    field, olon, olat, flon, flat = args
    fields = field.shape[0]
    values = field.reshape(fields, -1)
    spread = jnp.zeros_like(values)
    for target, weight in level_pairs(olon, olat, flon, flat):
        spread = spread.at[:, target].add(weight[None] * values)
    return spread.reshape(fields, NLON, NLAT)


def reference(increment, obs_dep, obs_weight, dep_lon, dep_lat, frac_lon, frac_lat, coupling):
    by_level = jnp.moveaxis(increment, 1, 0)
    advected = jnp.moveaxis(lax.map(forward_level, (by_level, dep_lon, dep_lat, frac_lon, frac_lat)), 0, 1)
    tl_out = column_solve(advected, coupling)
    forcing = obs_weight * (tl_out - obs_dep)
    smoothed = column_solve(forcing, coupling)
    adjoint = jnp.moveaxis(lax.map(backward_level, (jnp.moveaxis(smoothed, 1, 0), dep_lon, dep_lat, frac_lon, frac_lat)), 0, 1)
    gradient = increment + adjoint
    return (tl_out, gradient)
```

```python
import functools

import jax
import jax.numpy as jnp
from jax import lax
from jax.experimental import pallas as pl
from jax.experimental.pallas import tpu as pltpu
from jax.sharding import PartitionSpec as P

HALO = 6
SHIFTS = tuple(range(1 - HALO, HALO + 1))
LANES = 128
SLOT = 16
PER = LANES // SLOT
QUAD = 4
PAIR = 2
MESH = pl.DeviceIdType.MESH
ANY = pl.BlockSpec(memory_space=pl.ANY)
LIMIT = 56 * 1024 * 1024


def lane_index(shape):
    return lax.broadcasted_iota(jnp.int32, shape, len(shape) - 1)


def roll(x, shift):
    return pltpu.roll(x, shift, x.ndim - 1)


def neighbours(sizes):
    lat, lon = lax.axis_index("lat"), lax.axis_index("lon")

    def at(dy, dx):
        return {
            "lat": lax.rem(lat + dy + sizes[0], sizes[0]),
            "lon": lax.rem(lon + dx + sizes[1], sizes[1]),
        }

    return at


def greet(devices):
    barrier = pltpu.get_barrier_semaphore()
    for device in devices:
        pl.semaphore_signal(barrier, inc=1, device_id=device, device_id_type=MESH)
    pl.semaphore_wait(barrier, len(devices))


def remote(src, dst, send, recv, number, device):
    return pltpu.make_async_remote_copy(
        src_ref=src,
        dst_ref=dst,
        send_sem=send.at[number],
        recv_sem=recv.at[number],
        device_id=device,
        device_id_type=MESH,
    )


def pack_edges(src, base, dst):
    @pl.loop(0, dst.shape[0])
    def _(group):
        total = None
        for e in range(PER):
            x = src[base + group * PER + e]
            lane = lane_index(x.shape)
            x = jnp.where((lane < HALO) | (lane >= LANES - HALO), x, 0.0)
            x = roll(x, (HALO + SLOT * e) % LANES)
            total = x if total is None else total + x
        dst[group] = total


def pack_rows(src, base, low, high):
    @pl.loop(0, low.shape[0])
    def _(block):
        for i in range(QUAD):
            at = base + block * QUAD + i
            to = pl.ds(HALO * i, HALO)
            low[block, to] = src[at, 0:HALO].astype(jnp.float32)
            high[block, to] = src[at, 16 - HALO : 16].astype(jnp.float32)


def unpack_rows(src, base, left, right, dst):
    @pl.loop(0, left.shape[0])
    def _(block):
        for i in range(QUAD):
            at = block * QUAD + i
            of = pl.ds(HALO * i, HALO)
            dst[at, 8 - HALO : 8] = left[block, of]
            dst[at, 8:24] = src[base + at]
            dst[at, 24 : 24 + HALO] = right[block, of]


def store_weights(dst, rows, offset, frac):
    rest = 1.0 - frac
    before = None
    for pos, total in enumerate(SHIFTS):
        here = offset == total
        second = 0.0 if before is None else jnp.where(before, frac, 0.0)
        dst[pos, rows] = jnp.where(here, rest, second)
        before = here


def factor(dims, coup, ratio, inverse):
    fields, levels = dims
    previous = [None] * fields
    for k in range(levels):
        for f in range(fields):
            at, c = f * levels + k, f * (levels - 1) + k
            denom = 1.0
            if k > 0:
                below = coup[c - 1]
                denom = denom + below
            if k < levels - 1:
                above = coup[c]
                denom = denom + above
            if k > 0:
                denom = denom - below * previous[f]
            inv = 1.0 / denom
            inverse[at] = inv
            if k < levels - 1:
                previous[f] = above * inv
                ratio[at] = previous[f]


def advect(dims, first_field, band, bands, wide, edges, olon, olat, flon, flat, coup, inverse, shifted, prime):
    fields, levels = dims
    has_lower = band > 0
    has_upper = band < bands - 1

    @pl.loop(0, levels)
    def _(k):
        lane = lane_index(wide.shape[1:])
        for member in range(PAIR):
            local = member * levels + k
            group, slot = local // PER, local % PER
            shift = lax.rem(2 * LANES - HALO - SLOT * slot, LANES)
            lower = jnp.where(has_lower, roll(edges[0, group], shift), 0.0)
            upper = jnp.where(has_upper, roll(edges[1, group], shift), 0.0)
            shifted[member] = jnp.where(lane < LANES // 2, upper, lower)
        first = k == 0
        lane = lane_index((8, LANES))
        for half in range(2):
            rows = pl.ds(8 * half, 8)
            step, part = olon[k, rows], flon[k, rows]
            raw = [lane - olat[k, rows] - q for q in range(2)]
            index = [jnp.bitwise_and(x, LANES - 1) for x in raw]
            inside = [(x >= 0) & (x < LANES) for x in raw]
            evens, odds = jnp.bitwise_and(step + 1, -2), jnp.bitwise_or(step, 1)
            is_even = step == evens
            even_w = jnp.where(is_even, 1.0 - part, part)
            odd_w = jnp.where(is_even, part, 1.0 - part)
            one = flat[k, rows]
            zero = 1.0 - one
            for member in range(PAIR):
                local = member * levels + k
                found = {}
                for total in SHIFTS:
                    near = pl.ds(8 + 8 * half - total, 8)
                    here = (odds if total % 2 else evens) == total
                    for q in range(2):
                        x = jnp.take_along_axis(wide[local, near], index[q], axis=1)
                        e = jnp.take_along_axis(shifted[member, near], index[q], axis=1)
                        x = jnp.where(inside[q], x, e)
                        key = (total % 2, q)
                        found[key] = jnp.where(here, x, found[key]) if key in found else x
                value = even_w * (zero * found[0, 0] + one * found[0, 1])
                value = value + odd_w * (zero * found[1, 0] + one * found[1, 1])
                f = first_field + member
                at, c = f * levels + k, f * (levels - 1) + k
                below = jnp.where(first, 0.0, coup[jnp.where(first, c, c - 1), rows])
                before = jnp.where(first, 0.0, prime[jnp.where(first, at, at - 1), rows])
                prime[at, rows] = (value + below * before) * inverse[at, rows]


def solve(dims, first_field, prime, ratio, inverse, coup, dep, weight, tl, z):
    fields, levels = dims
    members = range(first_field, first_field + PAIR)
    x = {}
    for k in range(levels - 1, -1, -1):
        for f in members:
            at = f * levels + k
            x[f] = prime[at] if k == levels - 1 else prime[at] + ratio[at] * x[f]
            tl[at] = x[f]
    for k in range(levels):
        for f in members:
            at = f * levels + k
            forcing = weight[at] * (tl[at] - dep[at])
            if k > 0:
                forcing = forcing + coup[f * (levels - 1) + k - 1] * x[f]
            x[f] = forcing * inverse[at]
            prime[at] = x[f]
    for k in range(levels - 1, -1, -1):
        for f in members:
            at = f * levels + k
            x[f] = prime[at] if k == levels - 1 else prime[at] + ratio[at] * x[f]
            z[at] = x[f]


def collect(dims, first_field, wide, lonw, latw, inc, grad, spill):
    fields, levels = dims
    lane = lane_index((8, LANES))

    @pl.loop(0, levels)
    def _(k):
        for half in range(2):
            rows = pl.ds(8 * half, 8)
            sums = {}
            for lon_pos, lon_total in enumerate(SHIFTS):
                near = pl.ds(8 + 8 * half + lon_total, 8)
                scale = lonw[k, lon_pos, near]
                scaled = [scale * wide[f * levels + k, near] for f in range(PAIR)]
                for pos in range(len(SHIFTS)):
                    w = latw[k, pos, near]
                    for f in range(PAIR):
                        term = w * scaled[f]
                        sums[f, pos] = term if lon_pos == 0 else sums[f, pos] + term
            for f in range(PAIR):
                at = (first_field + f) * levels + k
                total, outside = inc[at, rows], jnp.zeros((8, LANES), jnp.float32)
                for pos, n in enumerate(SHIFTS):
                    if n == 0:
                        total = total + sums[f, pos]
                        continue
                    moved = roll(sums[f, pos], (-n) % LANES)
                    wraps = (lane >= LANES - n) if n > 0 else (lane < -n)
                    total = total + jnp.where(wraps, 0.0, moved)
                    outside = outside + jnp.where(wraps, moved, 0.0)
                grad[at, rows] = total
                spill[f * levels + k, rows] = outside


def finish(base, band, bands, edges, grad):
    has_lower = band > 0
    has_upper = band < bands - 1

    @pl.loop(0, edges.shape[1])
    def _(group):
        lower = jnp.where(has_lower, edges[0, group], 0.0)
        upper = jnp.where(has_upper, edges[1, group], 0.0)
        lane = lane_index(lower.shape)
        for e in range(PER):
            shift = (-HALO - SLOT * e) % LANES
            low = jnp.where(lane < HALO, roll(lower, shift), 0.0)
            high = jnp.where(lane >= LANES - HALO, roll(upper, shift), 0.0)
            at = base + group * PER + e
            grad[at] = grad[at] + (low + high)


def kernel(
    dims, sizes,
    inc_h, dep_h, weight_h, olon_h, olat_h, flon_h, flat_h, coup_h,
    tl_h, grad_h,
    inc, dep, weight, olon, olat, flon, flat, coup, tl, grad,
    low, high, from_left, from_right, edge_out, edge_in,
    g_low, g_high, g_left, g_right, z_low, z_high, z_left, z_right,
    back_out, back_in, spill, wide, shifted, lonw, latw, prime, ratio, inverse, z,
    load_sem, store_sem, send, recv,
):
    fields, levels = dims
    pairs = fields // PAIR
    per_pair = PAIR * levels
    at = neighbours(sizes)
    band, bands = lax.axis_index("lat"), sizes[0]
    numbers = iter(range(send.shape[0]))

    loads = [
        pltpu.make_async_copy(src, dst, load_sem.at[i])
        for i, (src, dst) in enumerate(
            [(inc_h, inc), (olon_h, olon), (olat_h, olat), (flon_h, flon), (flat_h, flat),
             (coup_h, coup), (dep_h, dep), (weight_h, weight)]
        )
    ]
    for load in loads:
        load.start()

    def launch(src, dst, device):
        copy = remote(src, dst, send, recv, next(numbers), device)
        copy.start()
        return copy

    greet([at(dy, dx) for dy in (-1, 0, 1) for dx in (-1, 0, 1) if (dy, dx) != (0, 0)])
    loads[0].wait()
    inward = []
    for pair in range(pairs):
        copies = []
        packed = edge_out.at[pair]
        pack_edges(inc, pair * per_pair, packed)
        for dy in (-1, 1):
            side = edge_in.at[pair, 0 if dy == 1 else 1]
            copies.append(launch(packed.at[:, 0:8], side.at[:, 24:32], at(dy, -1)))
            copies.append(launch(packed.at[:, 8:16], side.at[:, 0:8], at(dy, 1)))
            copies.append(launch(packed, side.at[:, 8:24], at(dy, 0)))
        pack_rows(inc, pair * per_pair, low.at[pair], high.at[pair])
        copies.append(launch(low.at[pair], from_right.at[pair], at(0, -1)))
        copies.append(launch(high.at[pair], from_left.at[pair], at(0, 1)))
        inward.append(copies)
    for load in loads[1:6]:
        load.wait()
    geometry = (olon, olat, flon, flat)
    blocks = levels // QUAD
    for i, own in enumerate(geometry):
        part = pl.ds(i * blocks, blocks)
        pack_rows(own, 0, g_low.at[part], g_high.at[part])
    around = [
        launch(g_low, g_right, at(0, -1)),
        launch(g_high, g_left, at(0, 1)),
    ]

    @pl.loop(0, levels)
    def _(k):
        store_weights(lonw.at[k], pl.ds(8, 16), olon[k], flon[k])
        store_weights(latw.at[k], pl.ds(8, 16), olat[k], flat[k])

    factor(dims, coup, ratio, inverse)
    for load in loads[6:]:
        load.wait()

    stores, across = [], []
    for pair in range(pairs):
        base = pair * per_pair
        for copy in inward[pair]:
            copy.wait()
        unpack_rows(inc, base, from_left.at[pair], from_right.at[pair], wide)
        advect(dims, pair * PAIR, band, bands, wide, edge_in.at[pair], olon, olat, flon, flat, coup, inverse, shifted, prime)
        solve(dims, pair * PAIR, prime, ratio, inverse, coup, dep, weight, tl, z)
        pack_rows(z, base, z_low.at[pair], z_high.at[pair])
        across.append([
            launch(z_low.at[pair], z_right.at[pair], at(0, -1)),
            launch(z_high.at[pair], z_left.at[pair], at(0, 1)),
        ])
        part = pl.ds(base, per_pair)
        store = pltpu.make_async_copy(tl.at[part], tl_h.at[part], store_sem.at[pair])
        store.start()
        stores.append(store)

    for copy in around:
        copy.wait()

    @pl.loop(0, blocks)
    def _(block):
        for i in range(QUAD):
            k = block * QUAD + i
            of = pl.ds(HALO * i, HALO)
            for side, rows in ((g_left, pl.ds(8 - HALO, HALO)), (g_right, pl.ds(24, HALO))):
                parts = [side[number * blocks + block, of] for number in range(4)]
                store_weights(lonw.at[k], rows, parts[0], parts[2])
                store_weights(latw.at[k], rows, parts[1], parts[3])

    returned = []
    for pair in range(pairs):
        base = pair * per_pair
        for copy in across[pair]:
            copy.wait()
        unpack_rows(z, base, z_left.at[pair], z_right.at[pair], wide)
        collect(dims, pair * PAIR, wide, lonw, latw, inc, grad, spill)
        pack_edges(spill, 0, back_out.at[pair])
        returned.append([
            launch(back_out.at[pair], back_in.at[pair, 1], at(-1, 0)),
            launch(back_out.at[pair], back_in.at[pair, 0], at(1, 0)),
        ])
    for pair in range(pairs):
        base = pair * per_pair
        for copy in returned[pair]:
            copy.wait()
        finish(base, band, bands, back_in.at[pair], grad)
        part = pl.ds(base, per_pair)
        store = pltpu.make_async_copy(grad.at[part], grad_h.at[part], store_sem.at[pairs + pair])
        store.start()
        stores.append(store)
    for store in stores:
        store.wait()


def shards(sizes, increment, obs_dep, obs_weight, dep_lon, dep_lat, frac_lon, frac_lat, coupling):
    fields, levels, rows, cols = increment.shape
    count = fields * levels
    pairs = fields // PAIR
    groups = PAIR * levels // PER
    quads = PAIR * levels // QUAD
    dims = (fields, levels)

    def vmem(*s, dtype=jnp.float32):
        return pltpu.VMEM(s, dtype)

    def flat3(x):
        return x.reshape(-1, rows, cols)

    whole = jax.ShapeDtypeStruct((count, rows, cols), jnp.float32)
    field = vmem(count, rows, cols)
    level = vmem(levels, rows, cols)
    index = vmem(levels, rows, cols, dtype=jnp.int32)
    halo = vmem(pairs, quads, QUAD * HALO, cols)
    g_halo = vmem(4 * levels // QUAD, QUAD * HALO, cols)
    weights = vmem(levels, len(SHIFTS), 32, cols)
    copies = pairs * 12 + 2
    tl, grad = pl.pallas_call(
        functools.partial(kernel, dims, sizes),
        out_shape=(whole, whole),
        in_specs=[ANY] * 8,
        out_specs=(ANY, ANY),
        scratch_shapes=[
            field, field, field, index, index, level, level,
            vmem(fields * (levels - 1), rows, cols), field, field,
            halo, halo, halo, halo,
            vmem(pairs, groups, rows, cols), vmem(pairs, 2, groups, 32, cols),
            g_halo, g_halo, g_halo, g_halo, halo, halo, halo, halo,
            vmem(pairs, groups, rows, cols), vmem(pairs, 2, groups, rows, cols),
            vmem(PAIR * levels, rows, cols), vmem(PAIR * levels, 32, cols),
            vmem(PAIR, 32, cols), weights, weights, field, field, field, field,
            pltpu.SemaphoreType.DMA((8,)),
            pltpu.SemaphoreType.DMA((2 * pairs,)),
            pltpu.SemaphoreType.DMA((copies,)),
            pltpu.SemaphoreType.DMA((copies,)),
        ],
        compiler_params=pltpu.CompilerParams(
            collective_id=0, has_side_effects=True, vmem_limit_bytes=LIMIT
        ),
    )(
        flat3(increment), flat3(obs_dep), flat3(obs_weight), dep_lon, dep_lat, frac_lon, frac_lat,
        flat3(coupling),
    )
    return tl.reshape(increment.shape), grad.reshape(increment.shape)


def solution(mesh):
    sizes = (mesh.shape["lat"], mesh.shape["lon"])
    wide = P(None, None, "lon", "lat")
    level = P(None, "lon", "lat")
    return jax.shard_map(
        functools.partial(shards, sizes),
        mesh=mesh,
        in_specs=(wide, wide, wide, level, level, level, level, wide),
        out_specs=(wide, wide),
        check_vma=False,
    )
```

```python
import functools

import jax
import jax.numpy as jnp
from jax import lax
from jax.experimental import pallas as pl
from jax.experimental.pallas import tpu as pltpu
from jax.sharding import PartitionSpec as P

HALO = 6
SHIFTS = tuple(range(1 - HALO, HALO + 1))
LANES = 128
SLOT = 16
PER = LANES // SLOT
TALL = 32
PAIR = 2
OUTER = (*range(HALO), *range(17 - HALO, 16))
MESH = pl.DeviceIdType.MESH
ANY = pl.BlockSpec(memory_space=pl.ANY)
LIMIT = 56 * 1024 * 1024


def lane_index(shape):
    return lax.broadcasted_iota(jnp.int32, shape, len(shape) - 1)


def roll(x, shift):
    return pltpu.roll(x, shift, x.ndim - 1)


def neighbours(sizes):
    lat, lon = lax.axis_index("lat"), lax.axis_index("lon")

    def at(dy, dx):
        return {
            "lat": lax.rem(lat + dy + sizes[0], sizes[0]),
            "lon": lax.rem(lon + dx + sizes[1], sizes[1]),
        }

    return at


def greet(devices):
    barrier = pltpu.get_barrier_semaphore()
    for device in devices:
        pl.semaphore_signal(barrier, inc=1, device_id=device, device_id_type=MESH)
    return lambda: pl.semaphore_wait(barrier, len(devices))


def remote(src, dst, send, recv, number, device):
    return pltpu.make_async_remote_copy(
        src_ref=src,
        dst_ref=dst,
        send_sem=send.at[number],
        recv_sem=recv.at[number],
        device_id=device,
        device_id_type=MESH,
    )


def tile(n, height=16):
    return pl.ds(pl.multiple_of(n * height, 8), height)


def pick(base, row, height):
    return pl.ds(base * height + row, 8, stride=height)


def edge_mask(lane):
    return (lane < HALO) | (lane >= LANES - HALO)


def pack_edges(load, dst):
    @pl.loop(0, dst.shape[0])
    def _(group):
        total = None
        for e in range(PER):
            x = load(group * PER + e)
            x = jnp.where(edge_mask(lane_index(x.shape)), x, jnp.zeros_like(x))
            x = roll(x, (HALO + SLOT * e) % LANES)
            total = x if total is None else total + x
        if dst.shape[1] == TALL:
            dst[group, 8:24] = total
        else:
            dst[group] = total


def weights(offset, frac):
    rest = 1.0 - frac
    before = None
    for total in SHIFTS:
        here = offset == total
        second = 0.0 if before is None else jnp.where(before, frac, 0.0)
        yield jnp.where(here, rest, second)
        before = here


def store_weights(dst, k, offset, frac):
    blank = jnp.zeros((8, LANES), jnp.float32)
    for pos, w in enumerate(weights(offset, frac)):
        dst[pos, pl.ds(k * TALL, 8)] = blank
        dst[pos, pl.ds(k * TALL + 8, 16)] = w
        dst[pos, pl.ds(k * TALL + 24, 8)] = blank


def store_across(levels, dst, offset, frac):
    @pl.loop(0, dst.shape[1])
    def _(group):
        level = lax.rem(group * PER, levels)
        for i, j in enumerate(OUTER):
            for pos, w in enumerate(weights(offset[pick(level, j, 16)], frac[pick(level, j, 16)])):
                dst[pos, group, i] = w


def factor(dims, coup, ratio, inverse):
    fields, levels = dims
    previous = [None] * fields
    for k in range(levels):
        for f in range(fields):
            at, c = f * levels + k, f * (levels - 1) + k
            denom = 1.0
            if k > 0:
                below = coup[c - 1]
                denom = denom + below
            if k < levels - 1:
                above = coup[c]
                denom = denom + above
            if k > 0:
                denom = denom - below * previous[f]
            inv = 1.0 / denom
            inverse[at] = inv
            if k < levels - 1:
                previous[f] = above * inv
                ratio[at] = previous[f]


def split_lon(step, part):
    evens, odds = jnp.bitwise_and(step + 1, -2), jnp.bitwise_or(step, 1)
    is_even = step == evens
    return (evens, odds), (jnp.where(is_even, 1.0 - part, part), jnp.where(is_even, part, 1.0 - part))


def interpolate(loads, half, index, lat_w, chosen, lon_w):
    found = {}
    masks = {total: chosen[total % 2] == total for total in SHIFTS}
    for q in range(2):
        for total in SHIFTS:
            near = 8 + 8 * half - total
            for m, load in enumerate(loads):
                x = jnp.take_along_axis(load(near), index[q], axis=1)
                key = (m, total % 2, q)
                found[key] = jnp.where(masks[total], x, found[key]) if key in found else x
    out = []
    for m in range(len(loads)):
        parts = [
            lon_w[o] * (lat_w[0] * found[m, o, 0] + lat_w[1] * found[m, o, 1]) for o in range(2)
        ]
        out.append(parts[0] + parts[1])
    return out


def advect(dims, base, wide, olon, olat, flon, flat, prime):
    fields, levels = dims
    lane = lane_index((8, LANES))

    @pl.loop(0, levels)
    def _(k):
        for half in range(2):
            rows = pl.ds(8 * half, 8)
            here = pl.ds(k * 16 + 8 * half, 8)
            raw = [lane - olat[here] - q for q in range(2)]
            index = [jnp.bitwise_and(x, LANES - 1) for x in raw]
            one = flat[here]
            lat_w = [
                jnp.where((x >= 0) & (x < LANES), w, 0.0) for x, w in zip(raw, (1.0 - one, one))
            ]
            chosen, lon_w = split_lon(olon[here], flon[here])
            loads = [
                lambda near, m=m: wide[base + m * levels + k, pl.ds(near, 8)] for m in range(PAIR)
            ]
            for m, x in enumerate(interpolate(loads, half, index, lat_w, chosen, lon_w)):
                prime[base + m * levels + k, rows] = x


def merge_edges(band, bands, edges, source):
    has_lower = band > 0
    has_upper = band < bands - 1

    @pl.loop(0, edges.shape[1])
    def _(group):
        slot = jnp.bitwise_and(lane_index((16, LANES)), SLOT - 1)
        lower = jnp.where(has_lower, edges[0, group], 0.0)
        upper = jnp.where(has_upper, edges[1, group], 0.0)
        source[group, 8:24] = jnp.where(slot < HALO, lower, upper)


def advect_edges(base, source, packed, result, prime):
    e_olon, e_olat, e_flon, e_flat = packed
    lane = lane_index((8, LANES))
    slot = jnp.bitwise_and(lane, SLOT - 1)

    @pl.loop(0, source.shape[0])
    def _(group):
        for half in range(2):
            rows = pl.ds(8 * half, 8)
            olat = e_olat[group, rows]
            one = e_flat[group, rows]
            index, lat_w = [], []
            for q, w in enumerate((1.0 - one, one)):
                near = slot - olat - q
                valid = ((slot < HALO) & (near >= HALO)) | (
                    (slot >= HALO) & (slot < 2 * HALO) & (near < HALO)
                )
                lat_w.append(jnp.where(valid, w, 0.0))
                index.append(jnp.bitwise_and(lane - olat - q, LANES - 1))
            chosen, lon_w = split_lon(e_olon[group, rows], e_flon[group, rows])
            loads = [lambda near: source[group, pl.ds(near, 8)]]
            result[group, rows] = interpolate(loads, half, index, lat_w, chosen, lon_w)[0]

    @pl.loop(0, source.shape[0])
    def _(group):
        x = result[group]
        keep = edge_mask(lane_index(x.shape))
        for e in range(PER):
            at = base + group * PER + e
            prime[at] = prime[at] + jnp.where(keep, roll(x, (-HALO - SLOT * e) % LANES), 0.0)


def solve(dims, first_field, prime, ratio, inverse, coup, dep, weight, tl, z):
    fields, levels = dims
    members = range(first_field, first_field + PAIR)
    x = {}
    for k in range(levels):
        for f in members:
            at = f * levels + k
            value = prime[at]
            if k > 0:
                value = value + coup[f * (levels - 1) + k - 1] * x[f]
            x[f] = value * inverse[at]
            prime[at] = x[f]
    for k in range(levels - 1, -1, -1):
        for f in members:
            at = f * levels + k
            x[f] = prime[at] if k == levels - 1 else prime[at] + ratio[at] * x[f]
            tl[at] = x[f]
    for k in range(levels):
        for f in members:
            at = f * levels + k
            forcing = weight[at] * (tl[at] - dep[at])
            if k > 0:
                forcing = forcing + coup[f * (levels - 1) + k - 1] * x[f]
            x[f] = forcing * inverse[at]
            prime[at] = x[f]
    for k in range(levels - 1, -1, -1):
        for f in members:
            at = f * levels + k
            x[f] = prime[at] if k == levels - 1 else prime[at] + ratio[at] * x[f]
            z[pl.ds(at * TALL + 8, 16)] = x[f]


def stay(x, n, lane):
    if n == 0:
        return x
    wraps = (lane >= LANES - n) if n > 0 else (lane < -n)
    return jnp.where(wraps, 0.0, roll(x, (-n) % LANES))


def spread_lon(dims, base, z, lonw, latw, low, high):
    levels = dims[1]
    lane = lane_index((8, LANES))

    @pl.loop(0, low.shape[0])
    def _(group):
        number = base + group * PER
        for out, targets, sources in (
            (low, range(-HALO, 0), range(HALO)),
            (high, range(16, 15 + HALO), range(17 - HALO, 16)),
        ):
            scaled = {}
            for j in sources:
                x = z[pick(number, 8 + j, TALL)]
                for a in targets:
                    if j - a in SHIFTS:
                        scaled[a, j] = x * lonw[SHIFTS.index(j - a), group, OUTER.index(j)]
            total = {}
            for pos, n in enumerate(SHIFTS):
                w = {j: latw[pos, group, OUTER.index(j)] for j in sources}
                for a in targets:
                    terms = [w[j] * scaled[a, j] for j in sources if (a, j) in scaled]
                    x = stay(functools.reduce(jnp.add, terms), n, lane)
                    total[a] = total[a] + x if a in total else x
            for e, a in enumerate(targets):
                out[group, e] = total[a]


def spread_edges(z, lonw, latw, result):
    slot = jnp.bitwise_and(lane_index((8, LANES)), SLOT - 1)

    @pl.loop(0, result.shape[0])
    def _(group):
        for part, steps in enumerate((range(1, HALO + 1), SHIFTS, SHIFTS, range(1 - HALO, 0))):
            sums = {}
            for r in steps:
                near = 8 * part + r
                scaled = lonw[SHIFTS.index(r), pl.ds(group * TALL + near, 8)] * z[group, pl.ds(near, 8)]
                for pos, n in enumerate(SHIFTS):
                    if n != 0:
                        term = latw[pos, pl.ds(group * TALL + near, 8)] * scaled
                        sums[n] = sums[n] + term if n in sums else term
            total = None
            for n, x in sums.items():
                if n > 0:
                    keep = (slot >= HALO - n) & (slot < HALO)
                else:
                    keep = (slot >= HALO) & (slot < HALO - n)
                x = jnp.where(keep, roll(x, (-n) % LANES), 0.0)
                total = x if total is None else total + x
            result[group, 8 * part : 8 * part + 8] = total


def add_corners(left, right, result):
    @pl.loop(0, result.shape[0])
    def _(group):
        row = lax.broadcasted_iota(jnp.int32, (8, LANES), 0)
        result[group, 8:16] = result[group, 8:16] + jnp.where(row < HALO - 1, left[group, 8:16], 0.0)
        result[group, 16:24] = result[group, 16:24] + jnp.where(row >= 8 - HALO, right[group, 16:24], 0.0)


def gather_lon(base, from_left, from_right, grad):
    @pl.loop(0, from_left.shape[0])
    def _(group):
        number = group * PER
        for side, first in ((from_right, 16 - HALO), (from_left, 0)):
            for e in range(side.shape[1]):
                at = pick(base + number, first + e, 16)
                grad[at] = grad[at] + side[group, e]


def collect(dims, base, z, lonw, latw, grad):
    levels = dims[1]
    lane = lane_index((8, LANES))

    @pl.loop(0, levels)
    def _(k):
        for half in range(2):
            sums = {}
            for lon_pos, lon_total in enumerate(SHIFTS):
                near = 8 + 8 * half + lon_total
                scale = lonw[lon_pos, pl.ds(k * TALL + near, 8)]
                scaled = [scale * z[pl.ds((base + f * levels + k) * TALL + near, 8)] for f in range(PAIR)]
                for pos in range(len(SHIFTS)):
                    w = latw[pos, pl.ds(k * TALL + near, 8)]
                    for f in range(PAIR):
                        term = w * scaled[f]
                        sums[f, pos] = term if lon_pos == 0 else sums[f, pos] + term
            for f in range(PAIR):
                at = pl.ds((base + f * levels + k) * 16 + 8 * half, 8)
                total = grad[at]
                for pos, n in enumerate(SHIFTS):
                    total = total + stay(sums[f, pos], n, lane)
                grad[at] = total


def finish(base, band, bands, edges, grad):
    has_lower = band > 0
    has_upper = band < bands - 1

    @pl.loop(0, edges.shape[1])
    def _(group):
        lower = jnp.where(has_lower, edges[0, group], 0.0)
        upper = jnp.where(has_upper, edges[1, group], 0.0)
        lane = lane_index(lower.shape)
        x = jnp.where(jnp.bitwise_and(lane, SLOT - 1) < HALO, upper, lower)
        keep = edge_mask(lane)
        for e in range(PER):
            at = tile(base + group * PER + e)
            grad[at] = grad[at] + jnp.where(keep, roll(x, (-HALO - SLOT * e) % LANES), 0.0)


def kernel(
    dims, sizes,
    inc_h, dep_h, weight_h, olon_h, olat_h, flon_h, flat_h, coup_h,
    tl_h, grad_h,
    wide, dep, weight, olon, olat, flon, flat, coup, tl, grad,
    edge_out, edge_in, e_source, e_result, e_olon, e_olat, e_flon, e_flat, e_lonw, e_latw, e_z,
    low, high, from_left, from_right, back_out, back_in, corner_left, corner_right,
    lonw, latw, t_lonw, t_latw, prime, ratio, inverse, z,
    load_sem, store_sem, send, recv,
):
    fields, levels = dims
    pairs = fields // PAIR
    per_pair = PAIR * levels
    at = neighbours(sizes)
    band, bands = lax.axis_index("lat"), sizes[0]
    has_lower = band > 0
    has_upper = band < bands - 1
    numbers = iter(range(send.shape[0]))

    copies = [
        (olon_h, olon), (olat_h, olat), (flon_h, flon), (flat_h, flat),
        (inc_h, wide.at[:, 8:24]), (coup_h, coup), (dep_h, dep), (weight_h, weight),
    ]
    spare = olon.shape[0] - levels * 16
    for src, dst in copies[:4]:
        copies.append((src.at[0:spare], dst.at[levels * 16 : levels * 16 + spare]))
    copies[:4] = [(src, dst.at[0 : levels * 16]) for src, dst in copies[:4]]
    loads = [pltpu.make_async_copy(src, dst, load_sem.at[i]) for i, (src, dst) in enumerate(copies)]
    for load in loads:
        load.start()

    def launch(src, dst, device):
        copy = remote(src, dst, send, recv, next(numbers), device)
        copy.start()
        return copy

    def launch_lat(src, dst):
        down = remote(src, dst.at[1], send, recv, next(numbers), at(-1, 0))
        up = remote(src, dst.at[0], send, recv, next(numbers), at(1, 0))
        pl.when(has_lower)(down.start)
        pl.when(has_upper)(up.start)
        return down, up

    def finish_lat(copies):
        down, up = copies
        pl.when(has_lower)(down.wait_send)
        pl.when(has_upper)(down.wait_recv)
        pl.when(has_upper)(up.wait_send)
        pl.when(has_lower)(up.wait_recv)

    meet = greet([at(-1, 0), at(1, 0), at(0, -1), at(0, 1)])
    loads[4].wait()
    for pair in range(pairs):
        base = pair * per_pair
        pack_edges(lambda n, base=base: wide[base + n, 8:24], edge_out.at[pair])
    meet()
    edges = [launch_lat(edge_out.at[pair], edge_in.at[pair]) for pair in range(pairs)]
    around = []
    for pair in range(pairs):
        part = pl.ds(pair * per_pair, per_pair)
        around.append([
            launch(inc_h.at[part, 0 : HALO - 1], wide.at[part, 24 : 23 + HALO], at(0, -1)),
            launch(inc_h.at[part, 16 - HALO : 16], wide.at[part, 8 - HALO : 8], at(0, 1)),
        ])

    def launch_corners(src, left, right, rows):
        return [launch(src.at[:, of], dst.at[:, to], device)
                for of, dst, to, device in zip(rows[0::2], (left, right), rows[1::2], (at(0, -1), at(0, 1)))]

    for load in (*loads[:4], *loads[8:]):
        load.wait()
    packed = (e_olon, e_olat, e_flon, e_flat)
    for src, dst in zip((olon, olat, flon, flat), packed):
        pack_edges(lambda n, src=src: src[tile(lax.rem(n, levels))], dst)
    store_across(levels, t_lonw, olon, flon)
    store_across(levels, t_latw, olat, flat)

    @pl.loop(0, levels)
    def _(k):
        store_weights(lonw, k, olon[tile(k)], flon[tile(k)])
        store_weights(latw, k, olat[tile(k)], flat[tile(k)])

    @pl.loop(0, e_olon.shape[0])
    def _(group):
        store_weights(e_lonw, group, e_olon[group], e_flon[group])
        store_weights(e_latw, group, e_olat[group], e_flat[group])
        e_z[group] = jnp.zeros((TALL, LANES), jnp.float32)

    @pl.loop(0, fields * levels)
    def _(n):
        z[pl.ds(n * TALL, 8)] = jnp.zeros((8, LANES), jnp.float32)
        z[pl.ds(n * TALL + 24, 8)] = jnp.zeros((8, LANES), jnp.float32)
        grad[tile(n)] = wide[n, 8:24]

    inner = []
    for pair in range(pairs):
        finish_lat(edges[pair])
        source = e_source.at[pair]
        merge_edges(band, bands, edge_in.at[pair], source)
        rows = (pl.ds(8, HALO - 1), pl.ds(24, HALO - 1), pl.ds(24 - HALO, HALO), pl.ds(8 - HALO, HALO))
        inner.append(launch_corners(source, source, source, rows))

    loads[5].wait()
    factor(dims, coup, ratio, inverse)
    for load in loads[6:8]:
        load.wait()

    stores, across, outer = [], [], []
    for pair in range(pairs):
        base = pair * per_pair
        for copy in around[pair]:
            copy.wait()
        advect(dims, base, wide, olon, olat, flon, flat, prime)
        for copy in inner[pair]:
            copy.wait()
        advect_edges(base, e_source.at[pair], packed, e_result, prime)
        solve(dims, pair * PAIR, prime, ratio, inverse, coup, dep, weight, tl, z)
        part = pl.ds(base, per_pair)
        store = pltpu.make_async_copy(tl.at[part], tl_h.at[part], store_sem.at[pair])
        store.start()
        stores.append(store)
        pack_edges(lambda n, base=base: z[pl.ds((base + n) * TALL + 8, 16)], e_z)
        spread_edges(e_z, e_lonw, e_latw, back_out.at[pair])
        rows = (pl.ds(8 - HALO, HALO), pl.ds(24 - HALO, HALO), pl.ds(24, HALO - 1), pl.ds(8, HALO - 1))
        outer.append(launch_corners(back_out.at[pair], corner_right.at[pair], corner_left.at[pair], rows))
        spread_lon(dims, base, z, t_lonw, t_latw, low.at[pair], high.at[pair])
        across.append([
            launch(low.at[pair], from_right.at[pair], at(0, -1)),
            launch(high.at[pair], from_left.at[pair], at(0, 1)),
        ])

    returned = []

    def pass_back(pair):
        for copy in outer[pair]:
            copy.wait()
        add_corners(corner_left.at[pair], corner_right.at[pair], back_out.at[pair])
        returned.append(launch_lat(back_out.at[pair, :, 8:24], back_in.at[pair]))

    def close(pair):
        base = pair * per_pair
        for copy in across[pair]:
            copy.wait()
        gather_lon(base, from_left.at[pair], from_right.at[pair], grad)
        finish_lat(returned[pair])
        finish(base, band, bands, back_in.at[pair], grad)

    for pair in range(pairs):
        base = pair * per_pair
        if pair == 0:
            pass_back(pair)
        else:
            close(pair)
        collect(dims, base, z, lonw, latw, grad)
        if pair == 0:
            for later in range(1, pairs):
                pass_back(later)
            close(pair)
        part = pl.ds(base * 16, per_pair * 16)
        store = pltpu.make_async_copy(grad.at[part], grad_h.at[part], store_sem.at[pairs + pair])
        store.start()
        stores.append(store)
    for store in stores:
        store.wait()


def shards(sizes, increment, obs_dep, obs_weight, dep_lon, dep_lat, frac_lon, frac_lat, coupling):
    fields, levels, rows, cols = increment.shape
    count = fields * levels
    pairs = fields // PAIR
    groups = PAIR * levels // PER
    spare = max(g * PER % levels for g in range(groups)) + PER - levels
    dims = (fields, levels)

    def vmem(*s, dtype=jnp.float32):
        return pltpu.VMEM(s, dtype)

    def flat2(x):
        return x.reshape(-1, cols)

    def flat3(x):
        return x.reshape(-1, rows, cols)

    field = vmem(count, rows, cols)
    level = vmem((levels + spare) * rows, cols)
    index = vmem((levels + spare) * rows, cols, dtype=jnp.int32)
    edge = vmem(groups, rows, cols)
    edge_index = vmem(groups, rows, cols, dtype=jnp.int32)
    edges = vmem(pairs, groups, TALL, cols)
    sides = vmem(pairs, 2, groups, rows, cols)
    low = vmem(pairs, groups, HALO, 8, cols)
    high = vmem(pairs, groups, HALO - 1, 8, cols)
    steps = len(SHIFTS)
    main_w = vmem(steps, levels * TALL, cols)
    edge_w = vmem(steps, groups * TALL, cols)
    outer_w = vmem(steps, groups, len(OUTER), PER, cols)
    copies = pairs * 12
    tl, grad = pl.pallas_call(
        functools.partial(kernel, dims, sizes),
        out_shape=(
            jax.ShapeDtypeStruct((count, rows, cols), jnp.float32),
            jax.ShapeDtypeStruct((count * rows, cols), jnp.float32),
        ),
        in_specs=[ANY] * 8,
        out_specs=(ANY, ANY),
        scratch_shapes=[
            vmem(count, TALL, cols), field, field, index, index, level, level,
            vmem(fields * (levels - 1), rows, cols), field, vmem(count * rows, cols),
            vmem(pairs, groups, rows, cols), sides, edges, edge,
            edge_index, edge_index, edge, edge, edge_w, edge_w, vmem(groups, TALL, cols),
            low, high, high, low, edges, sides, edges, edges,
            main_w, main_w, outer_w, outer_w, field, field, field, vmem(count * TALL, cols),
            pltpu.SemaphoreType.DMA((12,)),
            pltpu.SemaphoreType.DMA((2 * pairs,)),
            pltpu.SemaphoreType.DMA((copies,)),
            pltpu.SemaphoreType.DMA((copies,)),
        ],
        compiler_params=pltpu.CompilerParams(
            collective_id=0, has_side_effects=True, vmem_limit_bytes=LIMIT
        ),
    )(
        flat3(increment), flat3(obs_dep), flat3(obs_weight), flat2(dep_lon), flat2(dep_lat), flat2(frac_lon),
        flat2(frac_lat), flat3(coupling),
    )
    return tl.reshape(increment.shape), grad.reshape(increment.shape)


def solution(mesh):
    sizes = (mesh.shape["lat"], mesh.shape["lon"])
    wide = P(None, None, "lon", "lat")
    level = P(None, "lon", "lat")
    return jax.shard_map(
        functools.partial(shards, sizes),
        mesh=mesh,
        in_specs=(wide, wide, wide, level, level, level, level, wide),
        out_specs=(wide, wide),
        check_vma=False,
    )
```

```python
import functools

import jax
import jax.numpy as jnp
from jax import lax
from jax.experimental import pallas as pl
from jax.experimental.pallas import tpu as pltpu
from jax.sharding import PartitionSpec as P

HALO = 6
SHIFTS = tuple(range(1 - HALO, HALO + 1))
LANES = 128
SLOT = 16
PER = LANES // SLOT
TALL = 32
PAIR = 2
OUTER = (*range(HALO), *range(17 - HALO, 16))
UNROLL = 2
PARTS = 4
MESH = pl.DeviceIdType.MESH
ANY = pl.BlockSpec(memory_space=pl.ANY)
LIMIT = 56 * 1024 * 1024


def lane_index(shape):
    return lax.broadcasted_iota(jnp.int32, shape, len(shape) - 1)


def roll(x, shift):
    return pltpu.roll(x, shift, x.ndim - 1)


def neighbours(sizes):
    lat, lon = lax.axis_index("lat"), lax.axis_index("lon")

    def at(dy, dx):
        return {
            "lat": lax.rem(lat + dy + sizes[0], sizes[0]),
            "lon": lax.rem(lon + dx + sizes[1], sizes[1]),
        }

    return at


def greet(devices):
    barrier = pltpu.get_barrier_semaphore()
    for device in devices:
        pl.semaphore_signal(barrier, inc=1, device_id=device, device_id_type=MESH)
    return lambda: pl.semaphore_wait(barrier, len(devices))


def remote(src, dst, send, recv, number, device):
    return pltpu.make_async_remote_copy(
        src_ref=src,
        dst_ref=dst,
        send_sem=send.at[number],
        recv_sem=recv.at[number],
        device_id=device,
        device_id_type=MESH,
    )


def tile(n, height=16):
    return pl.ds(pl.multiple_of(n * height, 8), height)


def pick(base, row, height):
    return pl.ds(base * height + row, 8, stride=height)


def edge_mask(lane):
    return (lane < HALO) | (lane >= LANES - HALO)


def pack_edges(load, dst):
    for group in range(dst.shape[0]):
        total = None
        for e in range(PER):
            x = load(group * PER + e)
            x = jnp.where(edge_mask(lane_index(x.shape)), x, jnp.zeros_like(x))
            x = roll(x, (HALO + SLOT * e) % LANES)
            total = x if total is None else total + x
        if dst.shape[1] == TALL:
            dst[group, 8:24] = total
        else:
            dst[group] = total


def weights(offset, frac):
    rest = 1.0 - frac
    before = None
    for total in SHIFTS:
        here = offset == total
        second = 0.0 if before is None else jnp.where(before, frac, 0.0)
        yield total, jnp.where(here, rest, second)
        before = here


def lat_weights(offset, frac):
    lane = lane_index(frac.shape)
    for n, w in weights(offset, frac):
        yield n, w if n == 0 else jnp.where((lane >= n) if n > 0 else (lane < LANES + n), w, 0.0)


def edge_weights(offset, frac):
    high = jnp.bitwise_and(lane_index(frac.shape), SLOT - 1) < HALO
    by = dict(weights(offset, frac))
    for n in range(1, HALO + 1):
        yield n, jnp.where(high, by.get(-n, 0.0), by[n])


def store_weights(dst, k, values):
    blank = jnp.zeros((8, LANES), jnp.float32)
    for pos, (_, w) in enumerate(values):
        dst[pos, pl.ds(k * TALL, 8)] = blank
        dst[pos, pl.ds(k * TALL + 8, 16)] = w
        dst[pos, pl.ds(k * TALL + 24, 8)] = blank


def store_across(levels, dst, kind, offset, frac):
    @pl.loop(0, dst.shape[1])
    def _(group):
        level = lax.rem(group * PER, levels)
        for i, j in enumerate(OUTER):
            values = kind(offset[pick(level, j, 16)], frac[pick(level, j, 16)])
            for pos, (_, w) in enumerate(values):
                dst[pos, group, i] = w


def factor(dims, coup, ratio, inverse):
    fields, levels = dims
    previous = [None] * fields
    for k in range(levels):
        for f in range(fields):
            at, c = f * levels + k, f * (levels - 1) + k
            denom = 1.0
            if k > 0:
                below = coup[c - 1]
                denom = denom + below
            if k < levels - 1:
                above = coup[c]
                denom = denom + above
            if k > 0:
                denom = denom - below * previous[f]
            inv = 1.0 / denom
            inverse[at] = inv
            if k < levels - 1:
                previous[f] = above * inv
                ratio[at] = previous[f]


def split_lon(step, part):
    evens, odds = jnp.bitwise_and(step + 1, -2), jnp.bitwise_or(step, 1)
    is_even = step == evens
    return (evens, odds), (jnp.where(is_even, 1.0 - part, part), jnp.where(is_even, part, 1.0 - part))


def interpolate(loads, half, index, lat_w, chosen, lon_w, shifts):
    found = {}
    masks = {total: chosen[total % 2] == total for total in shifts}
    for q in range(2):
        for total in shifts:
            near = 8 + 8 * half - total
            for m, load in enumerate(loads):
                x = jnp.take_along_axis(load(near), index[q], axis=1)
                key = (m, total % 2, q)
                found[key] = jnp.where(masks[total], x, found.get(key, 0.0))
    out = []
    for m in range(len(loads)):
        parts = [
            lon_w[o] * (lat_w[0] * found[m, o, 0] + lat_w[1] * found[m, o, 1]) for o in range(2)
        ]
        out.append(parts[0] + parts[1])
    return out


def advect(dims, numbers, own, unroll, wide, olon, olat, flon, flat, prime):
    levels = dims[1]
    lane = lane_index((8, LANES))

    @pl.loop(0, levels // unroll)
    def _(block):
        for k in [block * unroll + i for i in range(unroll)]:
            for half in range(2):
                rows = pl.ds(8 * half, 8)
                here = pl.ds(k * 16 + 8 * half, 8)
                raw = [lane - olat[here] - q for q in range(2)]
                index = [jnp.bitwise_and(x, LANES - 1) for x in raw]
                one = flat[here]
                lat_w = [
                    jnp.where((x >= 0) & (x < LANES), w, 0.0) for x, w in zip(raw, (1.0 - one, one))
                ]
                chosen, lon_w = split_lon(olon[here], flon[here])
                shifts = [n for n in SHIFTS if own == (n <= 0 if half == 0 else n >= 0)]
                loads = [lambda near, f=f, k=k: wide[f * levels + k, pl.ds(near, 8)] for f in numbers]
                for f, x in zip(numbers, interpolate(loads, half, index, lat_w, chosen, lon_w, shifts)):
                    prime[f * levels + k, rows] = x if own else prime[f * levels + k, rows] + x


def merge_edges(band, bands, edges, source):
    has_lower = band > 0
    has_upper = band < bands - 1

    @pl.loop(0, edges.shape[1])
    def _(group):
        slot = jnp.bitwise_and(lane_index((16, LANES)), SLOT - 1)
        lower = jnp.where(has_lower, edges[0, group], 0.0)
        upper = jnp.where(has_upper, edges[1, group], 0.0)
        source[group, 8:24] = jnp.where(slot < HALO, lower, upper)


def advect_edges(base, source, packed, prime):
    e_olon, e_olat, e_flon, e_flat = packed
    lane = lane_index((8, LANES))
    slot = jnp.bitwise_and(lane, SLOT - 1)
    keep = edge_mask(lane)
    for group, half in [(group, half) for group in range(source.shape[0]) for half in range(2)]:
        rows = pl.ds(8 * half, 8)
        olat = e_olat[group, rows]
        one = e_flat[group, rows]
        index, lat_w = [], []
        for q, w in enumerate((1.0 - one, one)):
            near = slot - olat - q
            valid = ((slot < HALO) & (near >= HALO)) | (
                (slot >= HALO) & (slot < 2 * HALO) & (near < HALO)
            )
            lat_w.append(jnp.where(valid, w, 0.0))
            index.append(jnp.bitwise_and(lane - olat - q, LANES - 1))
        chosen, lon_w = split_lon(e_olon[group, rows], e_flon[group, rows])
        loads = [lambda near, group=group: source[group, pl.ds(near, 8)]]
        x = interpolate(loads, half, index, lat_w, chosen, lon_w, SHIFTS)[0]
        for e in range(PER):
            at = base + group * PER + e
            prime[at, rows] = prime[at, rows] + jnp.where(
                keep, roll(x, (-HALO - SLOT * e) % LANES), 0.0
            )


def solve(dims, first_field, prime, ratio, inverse, coup, dep, weight, tl, z):
    fields, levels = dims
    members = range(first_field, first_field + PAIR)
    x = {}
    for k in range(levels):
        for f in members:
            at = f * levels + k
            value = prime[at]
            if k > 0:
                value = value + coup[f * (levels - 1) + k - 1] * x[f]
            x[f] = value * inverse[at]
            prime[at] = x[f]
    for k in range(levels - 1, -1, -1):
        for f in members:
            at = f * levels + k
            x[f] = prime[at] if k == levels - 1 else prime[at] + ratio[at] * x[f]
            tl[at] = x[f]
    for k in range(levels):
        for f in members:
            at = f * levels + k
            forcing = weight[at] * (tl[at] - dep[at])
            if k > 0:
                forcing = forcing + coup[f * (levels - 1) + k - 1] * x[f]
            x[f] = forcing * inverse[at]
            prime[at] = x[f]
    for k in range(levels - 1, -1, -1):
        for f in members:
            at = f * levels + k
            x[f] = prime[at] if k == levels - 1 else prime[at] + ratio[at] * x[f]
            z[pl.ds(at * TALL + 8, 16)] = x[f]


def shifted(x, n):
    return x if n == 0 else roll(x, (-n) % LANES)


def spread_lon(dims, base, z, lonw, latw, low, high):
    @pl.loop(0, low.shape[0])
    def _(group):
        number = base + group * PER
        for out, targets, sources in (
            (low, range(-HALO, 0), range(HALO)),
            (high, range(16, 15 + HALO), range(17 - HALO, 16)),
        ):
            scaled = {}
            for j in sources:
                x = z[pick(number, 8 + j, TALL)]
                for a in targets:
                    if j - a in SHIFTS:
                        scaled[a, j] = x * lonw[SHIFTS.index(j - a), group, OUTER.index(j)]
            total = {}
            for pos, n in enumerate(SHIFTS):
                w = {j: latw[pos, group, OUTER.index(j)] for j in sources}
                for a in targets:
                    terms = [w[j] * scaled[a, j] for j in sources if (a, j) in scaled]
                    x = shifted(functools.reduce(jnp.add, terms), n)
                    total[a] = total[a] + x if a in total else x
            for e, a in enumerate(targets):
                out[group, e] = total[a]


def spread_edges(z, lonw, latw, result):
    slot = jnp.bitwise_and(lane_index((8, LANES)), SLOT - 1)

    @pl.loop(0, result.shape[0])
    def _(group):
        for part, steps in enumerate((range(1, HALO + 1), SHIFTS, SHIFTS, range(1 - HALO, 0))):
            sums = {}
            for r in steps:
                near = 8 * part + r
                scaled = lonw[SHIFTS.index(r), pl.ds(group * TALL + near, 8)] * z[group, pl.ds(near, 8)]
                for n in range(1, HALO + 1):
                    term = latw[n - 1, pl.ds(group * TALL + near, 8)] * scaled
                    sums[n] = sums[n] + term if n in sums else term
            total = None
            for n, x in sums.items():
                down = jnp.where((slot >= HALO - n) & (slot < HALO), shifted(x, n), 0.0)
                up = jnp.where((slot >= HALO) & (slot < HALO + n), shifted(x, -n), 0.0)
                total = down + up if total is None else total + (down + up)
            result[group, 8 * part : 8 * part + 8] = total


def add_corners(left, right, result):
    @pl.loop(0, result.shape[0])
    def _(group):
        row = lax.broadcasted_iota(jnp.int32, (8, LANES), 0)
        result[group, 8:16] = result[group, 8:16] + jnp.where(row < HALO - 1, left[group, 8:16], 0.0)
        result[group, 16:24] = result[group, 16:24] + jnp.where(row >= 8 - HALO, right[group, 16:24], 0.0)


def gather_lon(base, from_left, from_right, grad):
    @pl.loop(0, from_left.shape[0])
    def _(group):
        number = group * PER
        for side, first in ((from_right, 16 - HALO), (from_left, 0)):
            for e in range(side.shape[1]):
                at = pick(base + number, first + e, 16)
                grad[at] = grad[at] + side[group, e]


def collect(dims, base, z, lonw, latw, grad):
    levels = dims[1]

    @pl.loop(0, levels)
    def _(k):
        for half in range(2):
            sums = {}
            for lon_pos, lon_total in enumerate(SHIFTS):
                near = 8 + 8 * half + lon_total
                scale = lonw[lon_pos, pl.ds(k * TALL + near, 8)]
                scaled = [scale * z[pl.ds((base + f * levels + k) * TALL + near, 8)] for f in range(PAIR)]
                for pos in range(len(SHIFTS)):
                    w = latw[pos, pl.ds(k * TALL + near, 8)]
                    for f in range(PAIR):
                        term = w * scaled[f]
                        sums[f, pos] = term if lon_pos == 0 else sums[f, pos] + term
            for f in range(PAIR):
                at = pl.ds((base + f * levels + k) * 16 + 8 * half, 8)
                total = grad[at]
                for pos, n in enumerate(SHIFTS):
                    total = total + shifted(sums[f, pos], n)
                grad[at] = total


def finish(base, band, bands, edges, grad):
    has_lower = band > 0
    has_upper = band < bands - 1

    for group in range(edges.shape[1]):
        lower = jnp.where(has_lower, edges[0, group], 0.0)
        upper = jnp.where(has_upper, edges[1, group], 0.0)
        lane = lane_index(lower.shape)
        x = jnp.where(jnp.bitwise_and(lane, SLOT - 1) < HALO, upper, lower)
        keep = edge_mask(lane)
        for e in range(PER):
            at = tile(base + group * PER + e)
            grad[at] = grad[at] + jnp.where(keep, roll(x, (-HALO - SLOT * e) % LANES), 0.0)


def kernel(
    dims, sizes,
    inc_h, dep_h, weight_h, olon_h, olat_h, flon_h, flat_h, coup_h,
    tl_h, grad_h,
    wide, dep, weight, olon, olat, flon, flat, coup, tl, grad,
    edge_out, edge_in, e_source, e_olon, e_olat, e_flon, e_flat, e_lonw, e_latw, e_z,
    low, high, from_left, from_right, back_out, back_in, corner_left, corner_right,
    lonw, latw, t_lonw, t_latw, prime, ratio, inverse, z,
    load_sem, store_sem, send, recv,
):
    fields, levels = dims
    pairs = fields // PAIR
    per_pair = PAIR * levels
    at = neighbours(sizes)
    band, bands = lax.axis_index("lat"), sizes[0]
    has_lower = band > 0
    has_upper = band < bands - 1
    numbers = iter(range(send.shape[0]))

    copies = [
        (olon_h, olon), (olat_h, olat), (flon_h, flon), (flat_h, flat),
        (inc_h, wide.at[:, 8:24]), (coup_h, coup), (dep_h, dep), (weight_h, weight),
    ]
    spare = olon.shape[0] - levels * 16
    for src, dst in copies[:4]:
        copies.append((src.at[0:spare], dst.at[levels * 16 : levels * 16 + spare]))
    copies[:4] = [(src, dst.at[0 : levels * 16]) for src, dst in copies[:4]]
    loads = [pltpu.make_async_copy(src, dst, load_sem.at[i]) for i, (src, dst) in enumerate(copies)]
    for load in loads:
        load.start()

    def launch(src, dst, device):
        copy = remote(src, dst, send, recv, next(numbers), device)
        copy.start()
        return copy

    def launch_lat(src, dst):
        down = remote(src, dst.at[1], send, recv, next(numbers), at(-1, 0))
        up = remote(src, dst.at[0], send, recv, next(numbers), at(1, 0))
        pl.when(has_lower)(down.start)
        pl.when(has_upper)(up.start)
        return down, up

    def finish_lat(copies):
        down, up = copies
        pl.when(has_lower)(down.wait_send)
        pl.when(has_upper)(down.wait_recv)
        pl.when(has_upper)(up.wait_send)
        pl.when(has_lower)(up.wait_recv)

    meet = greet([at(-1, 0), at(1, 0), at(0, -1), at(0, 1)])
    loads[4].wait()
    for pair in range(pairs):
        base = pair * per_pair
        pack_edges(lambda n, base=base: wide[base + n, 8:24], edge_out.at[pair])
    for load in (*loads[:4], *loads[8:]):
        load.wait()
    packed = (e_olon, e_olat, e_flon, e_flat)
    for src, dst in zip((olon, olat, flon, flat), packed):
        pack_edges(lambda n, src=src: src[pl.ds(n % levels * 16, 16)], dst)
    meet()
    edges = [launch_lat(edge_out.at[pair], edge_in.at[pair]) for pair in range(pairs)]
    around = []
    for pair in range(pairs):
        part = pl.ds(pair * per_pair, per_pair)
        around.append([
            launch(inc_h.at[part, 0 : HALO - 1], wide.at[part, 24 : 23 + HALO], at(0, -1)),
            launch(inc_h.at[part, 16 - HALO : 16], wide.at[part, 8 - HALO : 8], at(0, 1)),
        ])

    def launch_corners(src, left, right, rows):
        return [launch(src.at[:, of], dst.at[:, to], device)
                for of, dst, to, device in zip(rows[0::2], (left, right), rows[1::2], (at(0, -1), at(0, 1)))]

    store_across(levels, t_lonw, weights, olon, flon)
    store_across(levels, t_latw, lat_weights, olat, flat)

    @pl.loop(0, levels)
    def _(k):
        store_weights(lonw, k, weights(olon[tile(k)], flon[tile(k)]))
        store_weights(latw, k, lat_weights(olat[tile(k)], flat[tile(k)]))

    @pl.loop(0, e_olon.shape[0])
    def _(group):
        store_weights(e_lonw, group, weights(e_olon[group], e_flon[group]))
        store_weights(e_latw, group, edge_weights(e_olat[group], e_flat[group]))
        e_z[group] = jnp.zeros((TALL, LANES), jnp.float32)

    @pl.loop(0, fields * levels)
    def _(n):
        z[pl.ds(n * TALL, 8)] = jnp.zeros((8, LANES), jnp.float32)
        z[pl.ds(n * TALL + 24, 8)] = jnp.zeros((8, LANES), jnp.float32)
        grad[tile(n)] = wide[n, 8:24]

    inner = []
    for pair in range(pairs):
        finish_lat(edges[pair])
        source = e_source.at[pair]
        merge_edges(band, bands, edge_in.at[pair], source)
        rows = (pl.ds(8, HALO - 1), pl.ds(24, HALO - 1), pl.ds(24 - HALO, HALO), pl.ds(8 - HALO, HALO))
        inner.append(launch_corners(source, source, source, rows))

    advect(dims, range(fields), True, UNROLL, wide, olon, olat, flon, flat, prime)
    loads[5].wait()
    factor(dims, coup, ratio, inverse)
    for load in loads[6:8]:
        load.wait()

    stores, across, outer = [], [], []
    for pair in range(pairs):
        base = pair * per_pair
        for copy in around[pair]:
            copy.wait()
        members = range(pair * PAIR, pair * PAIR + PAIR)
        advect(dims, members, False, 2 * UNROLL, wide, olon, olat, flon, flat, prime)
        for copy in inner[pair]:
            copy.wait()
        advect_edges(base, e_source.at[pair], packed, prime)
        solve(dims, pair * PAIR, prime, ratio, inverse, coup, dep, weight, tl, z)
        part = pl.ds(base, per_pair)
        store = pltpu.make_async_copy(tl.at[part], tl_h.at[part], store_sem.at[pair])
        store.start()
        stores.append(store)
        pack_edges(lambda n, base=base: z[pl.ds((base + n) * TALL + 8, 16)], e_z)
        spread_edges(e_z, e_lonw, e_latw, back_out.at[pair])
        rows = (pl.ds(8 - HALO, HALO), pl.ds(24 - HALO, HALO), pl.ds(24, HALO - 1), pl.ds(8, HALO - 1))
        outer.append(launch_corners(back_out.at[pair], corner_right.at[pair], corner_left.at[pair], rows))
        spread_lon(dims, base, z, t_lonw, t_latw, low.at[pair], high.at[pair])
        across.append([
            launch(low.at[pair], from_right.at[pair], at(0, -1)),
            launch(high.at[pair], from_left.at[pair], at(0, 1)),
        ])

    returned = []

    def pass_back(pair):
        for copy in outer[pair]:
            copy.wait()
        add_corners(corner_left.at[pair], corner_right.at[pair], back_out.at[pair])
        returned.append(launch_lat(back_out.at[pair, :, 8:24], back_in.at[pair]))

    def close(pair):
        base = pair * per_pair
        for copy in across[pair]:
            copy.wait()
        gather_lon(base, from_left.at[pair], from_right.at[pair], grad)
        finish_lat(returned[pair])
        finish(base, band, bands, back_in.at[pair], grad)

    for pair in range(pairs):
        base = pair * per_pair
        if pair == 0:
            pass_back(pair)
        else:
            close(pair)
        collect(dims, base, z, lonw, latw, grad)
        if pair == 0:
            for later in range(1, pairs):
                pass_back(later)
            close(pair)
        part = pl.ds(base * 16, per_pair * 16)
        store = pltpu.make_async_copy(grad.at[part], grad_h.at[part], store_sem.at[pairs + pair])
        store.start()
        stores.append(store)
    for store in stores:
        store.wait()


def place(a_h, b_h, a_o, b_o, a, b, sem):
    moves = []
    for i in range(PARTS):
        for j, (src, mid, dst) in enumerate(((a_h, a, a_o), (b_h, b, b_o))):
            size = src.shape[0] // PARTS
            part = pl.ds(i * size, size)
            moves.append((
                pltpu.make_async_copy(src.at[part], mid.at[part], sem.at[0, 2 * i + j]),
                pltpu.make_async_copy(mid.at[part], dst.at[part], sem.at[1, 2 * i + j]),
            ))
    for first, _ in moves:
        first.start()
    for first, then in moves:
        first.wait()
        then.start()
    for _, then in moves:
        then.wait()


def shards(sizes, increment, obs_dep, obs_weight, dep_lon, dep_lat, frac_lon, frac_lat, coupling):
    fields, levels, rows, cols = increment.shape
    count = fields * levels
    pairs = fields // PAIR
    groups = PAIR * levels // PER
    spare = max(g * PER % levels for g in range(groups)) + PER - levels
    dims = (fields, levels)

    def vmem(*s, dtype=jnp.float32):
        return pltpu.VMEM(s, dtype)

    def flat2(x):
        return x.reshape(-1, cols)

    def flat3(x):
        return x.reshape(-1, rows, cols)

    field = vmem(count, rows, cols)
    level = vmem((levels + spare) * rows, cols)
    index = vmem((levels + spare) * rows, cols, dtype=jnp.int32)
    edge = vmem(groups, rows, cols)
    edge_index = vmem(groups, rows, cols, dtype=jnp.int32)
    edges = vmem(pairs, groups, TALL, cols)
    sides = vmem(pairs, 2, groups, rows, cols)
    low = vmem(pairs, groups, HALO, 8, cols)
    high = vmem(pairs, groups, HALO - 1, 8, cols)
    steps = len(SHIFTS)
    main_w = vmem(steps, levels * TALL, cols)
    edge_w = vmem(steps, groups * TALL, cols)
    outer_w = vmem(steps, groups, len(OUTER), PER, cols)
    copies = pairs * 12
    tl, grad = pl.pallas_call(
        functools.partial(kernel, dims, sizes),
        out_shape=(
            jax.ShapeDtypeStruct((count, rows, cols), jnp.float32),
            jax.ShapeDtypeStruct((count * rows, cols), jnp.float32),
        ),
        in_specs=[ANY] * 8,
        out_specs=(ANY, ANY),
        scratch_shapes=[
            vmem(count, TALL, cols), field, field, index, index, level, level,
            vmem(fields * (levels - 1), rows, cols), field, vmem(count * rows, cols),
            vmem(pairs, groups, rows, cols), sides, edges,
            edge_index, edge_index, edge, edge, edge_w, vmem(HALO, groups * TALL, cols), vmem(groups, TALL, cols),
            low, high, high, low, edges, sides, edges, edges,
            main_w, main_w, outer_w, outer_w, field, field, field, vmem(count * TALL, cols),
            pltpu.SemaphoreType.DMA((12,)),
            pltpu.SemaphoreType.DMA((2 * pairs,)),
            pltpu.SemaphoreType.DMA((copies,)),
            pltpu.SemaphoreType.DMA((copies,)),
        ],
        compiler_params=pltpu.CompilerParams(
            collective_id=0, has_side_effects=True, vmem_limit_bytes=LIMIT
        ),
    )(
        flat3(increment), flat3(obs_dep), flat3(obs_weight), flat2(dep_lon), flat2(dep_lat), flat2(frac_lon),
        flat2(frac_lat), flat3(coupling),
    )
    tl, grad = pl.pallas_call(
        place,
        out_shape=tuple(jax.ShapeDtypeStruct(x.shape, x.dtype) for x in (tl, grad)),
        in_specs=[ANY] * 2,
        out_specs=(ANY, ANY),
        scratch_shapes=[
            vmem(*tl.shape), vmem(*grad.shape), pltpu.SemaphoreType.DMA((2, 2 * PARTS))
        ],
        compiler_params=pltpu.CompilerParams(vmem_limit_bytes=LIMIT),
    )(tl, grad)
    return tl.reshape(increment.shape), grad.reshape(increment.shape)


def solution(mesh):
    sizes = (mesh.shape["lat"], mesh.shape["lon"])
    wide = P(None, None, "lon", "lat")
    level = P(None, "lon", "lat")
    return jax.shard_map(
        functools.partial(shards, sizes),
        mesh=mesh,
        in_specs=(wide, wide, wide, level, level, level, level, wide),
        out_specs=(wide, wide),
        check_vma=False,
    )
```

```python
import functools

import jax
import jax.numpy as jnp
from jax import lax
from jax.experimental import pallas as pl
from jax.experimental.pallas import tpu as pltpu
from jax.sharding import PartitionSpec as P

HALO = 6
SHIFTS = tuple(range(1 - HALO, HALO + 1))
LANES = 128
SLOT = 16
PER = LANES // SLOT
TALL = 32
PAIR = 2
OUTER = (*range(HALO), *range(17 - HALO, 16))
UNROLL = 2
MESH = pl.DeviceIdType.MESH
ANY = pl.BlockSpec(memory_space=pl.ANY)
WITHIN = pl.BlockSpec(memory_space=pltpu.VMEM)
LIMIT = 44 * 1024 * 1024


def lane_index(shape):
    return lax.broadcasted_iota(jnp.int32, shape, len(shape) - 1)


def roll(x, shift):
    return pltpu.roll(x, shift, x.ndim - 1)


def neighbours(sizes):
    lat, lon = lax.axis_index("lat"), lax.axis_index("lon")

    def at(dy, dx):
        return {
            "lat": lax.rem(lat + dy + sizes[0], sizes[0]),
            "lon": lax.rem(lon + dx + sizes[1], sizes[1]),
        }

    return at


def greet(devices):
    barrier = pltpu.get_barrier_semaphore()
    for device in devices:
        pl.semaphore_signal(barrier, inc=1, device_id=device, device_id_type=MESH)
    return lambda: pl.semaphore_wait(barrier, len(devices))


def remote(src, dst, send, recv, number, device):
    return pltpu.make_async_remote_copy(
        src_ref=src,
        dst_ref=dst,
        send_sem=send.at[number],
        recv_sem=recv.at[number],
        device_id=device,
        device_id_type=MESH,
    )


def tile(n, height=16):
    return pl.ds(pl.multiple_of(n * height, 8), height)


def pick(base, row, height):
    return pl.ds(base * height + row, 8, stride=height)


def edge_mask(lane):
    return (lane < HALO) | (lane >= LANES - HALO)


def pack_edges(load, dst):
    for group in range(dst.shape[0]):
        total = None
        for e in range(PER):
            x = load(group * PER + e)
            x = jnp.where(edge_mask(lane_index(x.shape)), x, jnp.zeros_like(x))
            x = roll(x, (HALO + SLOT * e) % LANES)
            total = x if total is None else total + x
        if dst.shape[1] == TALL:
            dst[group, 8:24] = total
        else:
            dst[group] = total


def weights(offset, frac):
    rest = 1.0 - frac
    before = None
    for total in SHIFTS:
        here = offset == total
        second = 0.0 if before is None else jnp.where(before, frac, 0.0)
        yield total, jnp.where(here, rest, second)
        before = here


def lat_weights(offset, frac):
    lane = lane_index(frac.shape)
    for n, w in weights(offset, frac):
        yield n, w if n == 0 else jnp.where((lane >= n) if n > 0 else (lane < LANES + n), w, 0.0)


def edge_weights(offset, frac):
    high = jnp.bitwise_and(lane_index(frac.shape), SLOT - 1) < HALO
    by = dict(weights(offset, frac))
    for n in range(1, HALO + 1):
        yield n, jnp.where(high, by.get(-n, 0.0), by[n])


def store_weights(dst, k, values):
    blank = jnp.zeros((8, LANES), jnp.float32)
    for pos, (_, w) in enumerate(values):
        dst[pos, pl.ds(k * TALL, 8)] = blank
        dst[pos, pl.ds(k * TALL + 8, 16)] = w
        dst[pos, pl.ds(k * TALL + 24, 8)] = blank


def store_across(levels, dst, kind, offset, frac):
    @pl.loop(0, dst.shape[1])
    def _(group):
        level = lax.rem(group * PER, levels)
        for i, j in enumerate(OUTER):
            values = kind(offset[pick(level, j, 16)], frac[pick(level, j, 16)])
            for pos, (_, w) in enumerate(values):
                dst[pos, group, i] = w


def factor(dims, coup, ratio, inverse):
    fields, levels = dims
    previous = [None] * fields
    for k in range(levels):
        for f in range(fields):
            at, c = f * levels + k, f * (levels - 1) + k
            denom = 1.0
            if k > 0:
                below = coup[c - 1]
                denom = denom + below
            if k < levels - 1:
                above = coup[c]
                denom = denom + above
            if k > 0:
                denom = denom - below * previous[f]
            inv = 1.0 / denom
            inverse[at] = inv
            if k < levels - 1:
                previous[f] = above * inv
                ratio[at] = previous[f]


def split_lon(step, part):
    evens, odds = jnp.bitwise_and(step + 1, -2), jnp.bitwise_or(step, 1)
    is_even = step == evens
    return (evens, odds), (jnp.where(is_even, 1.0 - part, part), jnp.where(is_even, part, 1.0 - part))


def interpolate(loads, half, index, lat_w, chosen, lon_w, shifts):
    found = {}
    masks = {total: chosen[total % 2] == total for total in shifts}
    for q in range(2):
        for total in shifts:
            near = 8 + 8 * half - total
            for m, load in enumerate(loads):
                x = jnp.take_along_axis(load(near), index[q], axis=1)
                key = (m, total % 2, q)
                found[key] = jnp.where(masks[total], x, found.get(key, 0.0))
    out = []
    for m in range(len(loads)):
        parts = [
            lon_w[o] * (lat_w[0] * found[m, o, 0] + lat_w[1] * found[m, o, 1]) for o in range(2)
        ]
        out.append(parts[0] + parts[1])
    return out


def advect(dims, numbers, own, unroll, wide, olon, olat, flon, flat, prime):
    levels = dims[1]
    lane = lane_index((8, LANES))

    @pl.loop(0, levels // unroll)
    def _(block):
        for k in [block * unroll + i for i in range(unroll)]:
            for half in range(2):
                rows = pl.ds(8 * half, 8)
                here = pl.ds(k * 16 + 8 * half, 8)
                raw = [lane - olat[here] - q for q in range(2)]
                index = [jnp.bitwise_and(x, LANES - 1) for x in raw]
                one = flat[here]
                lat_w = [
                    jnp.where((x >= 0) & (x < LANES), w, 0.0) for x, w in zip(raw, (1.0 - one, one))
                ]
                chosen, lon_w = split_lon(olon[here], flon[here])
                shifts = [n for n in SHIFTS if own == (n <= 0 if half == 0 else n >= 0)]
                loads = [lambda near, f=f, k=k: wide[f * levels + k, pl.ds(near, 8)] for f in numbers]
                for f, x in zip(numbers, interpolate(loads, half, index, lat_w, chosen, lon_w, shifts)):
                    prime[f * levels + k, rows] = x if own else prime[f * levels + k, rows] + x


def merge_edges(band, bands, edges, source):
    has_lower = band > 0
    has_upper = band < bands - 1

    @pl.loop(0, edges.shape[1])
    def _(group):
        slot = jnp.bitwise_and(lane_index((16, LANES)), SLOT - 1)
        lower = jnp.where(has_lower, edges[0, group], 0.0)
        upper = jnp.where(has_upper, edges[1, group], 0.0)
        source[group, 8:24] = jnp.where(slot < HALO, lower, upper)


def advect_edges(base, source, packed, prime):
    e_olon, e_olat, e_flon, e_flat = packed
    lane = lane_index((8, LANES))
    slot = jnp.bitwise_and(lane, SLOT - 1)
    keep = edge_mask(lane)
    for group, half in [(group, half) for group in range(source.shape[0]) for half in range(2)]:
        rows = pl.ds(8 * half, 8)
        olat = e_olat[group, rows]
        one = e_flat[group, rows]
        index, lat_w = [], []
        for q, w in enumerate((1.0 - one, one)):
            near = slot - olat - q
            valid = ((slot < HALO) & (near >= HALO)) | (
                (slot >= HALO) & (slot < 2 * HALO) & (near < HALO)
            )
            lat_w.append(jnp.where(valid, w, 0.0))
            index.append(jnp.bitwise_and(lane - olat - q, LANES - 1))
        chosen, lon_w = split_lon(e_olon[group, rows], e_flon[group, rows])
        loads = [lambda near, group=group: source[group, pl.ds(near, 8)]]
        x = interpolate(loads, half, index, lat_w, chosen, lon_w, SHIFTS)[0]
        for e in range(PER):
            at = base + group * PER + e
            prime[at, rows] = prime[at, rows] + jnp.where(
                keep, roll(x, (-HALO - SLOT * e) % LANES), 0.0
            )


def solve(dims, first_field, prime, ratio, inverse, coup, dep, weight, tl, z):
    fields, levels = dims
    members = range(first_field, first_field + PAIR)
    x = {}
    for k in range(levels):
        for f in members:
            at = f * levels + k
            value = prime[at]
            if k > 0:
                value = value + coup[f * (levels - 1) + k - 1] * x[f]
            x[f] = value * inverse[at]
            prime[at] = x[f]
    for k in range(levels - 1, -1, -1):
        for f in members:
            at = f * levels + k
            x[f] = prime[at] if k == levels - 1 else prime[at] + ratio[at] * x[f]
            tl[at] = x[f]
    for k in range(levels):
        for f in members:
            at = f * levels + k
            forcing = weight[at] * (tl[at] - dep[at])
            if k > 0:
                forcing = forcing + coup[f * (levels - 1) + k - 1] * x[f]
            x[f] = forcing * inverse[at]
            prime[at] = x[f]
    for k in range(levels - 1, -1, -1):
        for f in members:
            at = f * levels + k
            x[f] = prime[at] if k == levels - 1 else prime[at] + ratio[at] * x[f]
            z[pl.ds(at * TALL + 8, 16)] = x[f]


def shifted(x, n):
    return x if n == 0 else roll(x, (-n) % LANES)


def spread_lon(dims, base, z, lonw, latw, low, high):
    @pl.loop(0, low.shape[0])
    def _(group):
        number = base + group * PER
        for out, targets, sources in (
            (low, range(-HALO, 0), range(HALO)),
            (high, range(16, 15 + HALO), range(17 - HALO, 16)),
        ):
            scaled = {}
            for j in sources:
                x = z[pick(number, 8 + j, TALL)]
                for a in targets:
                    if j - a in SHIFTS:
                        scaled[a, j] = x * lonw[SHIFTS.index(j - a), group, OUTER.index(j)]
            total = {}
            for pos, n in enumerate(SHIFTS):
                w = {j: latw[pos, group, OUTER.index(j)] for j in sources}
                for a in targets:
                    terms = [w[j] * scaled[a, j] for j in sources if (a, j) in scaled]
                    x = shifted(functools.reduce(jnp.add, terms), n)
                    total[a] = total[a] + x if a in total else x
            for e, a in enumerate(targets):
                out[group, e] = total[a]


def spread_edges(z, lonw, latw, result):
    slot = jnp.bitwise_and(lane_index((8, LANES)), SLOT - 1)

    @pl.loop(0, result.shape[0])
    def _(group):
        for part, steps in enumerate((range(1, HALO + 1), SHIFTS, SHIFTS, range(1 - HALO, 0))):
            sums = {}
            for r in steps:
                near = 8 * part + r
                scaled = lonw[SHIFTS.index(r), pl.ds(group * TALL + near, 8)] * z[group, pl.ds(near, 8)]
                for n in range(1, HALO + 1):
                    term = latw[n - 1, pl.ds(group * TALL + near, 8)] * scaled
                    sums[n] = sums[n] + term if n in sums else term
            total = None
            for n, x in sums.items():
                down = jnp.where((slot >= HALO - n) & (slot < HALO), shifted(x, n), 0.0)
                up = jnp.where((slot >= HALO) & (slot < HALO + n), shifted(x, -n), 0.0)
                total = down + up if total is None else total + (down + up)
            result[group, 8 * part : 8 * part + 8] = total


def add_corners(left, right, result):
    @pl.loop(0, result.shape[0])
    def _(group):
        row = lax.broadcasted_iota(jnp.int32, (8, LANES), 0)
        result[group, 8:16] = result[group, 8:16] + jnp.where(row < HALO - 1, left[group, 8:16], 0.0)
        result[group, 16:24] = result[group, 16:24] + jnp.where(row >= 8 - HALO, right[group, 16:24], 0.0)


def gather_lon(base, from_left, from_right, grad):
    @pl.loop(0, from_left.shape[0])
    def _(group):
        number = group * PER
        for side, first in ((from_right, 16 - HALO), (from_left, 0)):
            for e in range(side.shape[1]):
                at = pick(base + number, first + e, 16)
                grad[at] = grad[at] + side[group, e]


def collect(dims, base, z, lonw, latw, grad):
    levels = dims[1]

    @pl.loop(0, levels)
    def _(k):
        for half in range(2):
            sums = {}
            for lon_pos, lon_total in enumerate(SHIFTS):
                near = 8 + 8 * half + lon_total
                scale = lonw[lon_pos, pl.ds(k * TALL + near, 8)]
                scaled = [scale * z[pl.ds((base + f * levels + k) * TALL + near, 8)] for f in range(PAIR)]
                for pos in range(len(SHIFTS)):
                    w = latw[pos, pl.ds(k * TALL + near, 8)]
                    for f in range(PAIR):
                        term = w * scaled[f]
                        sums[f, pos] = term if lon_pos == 0 else sums[f, pos] + term
            for f in range(PAIR):
                at = pl.ds((base + f * levels + k) * 16 + 8 * half, 8)
                total = grad[at]
                for pos, n in enumerate(SHIFTS):
                    total = total + shifted(sums[f, pos], n)
                grad[at] = total


def finish(base, band, bands, edges, grad):
    has_lower = band > 0
    has_upper = band < bands - 1

    for group in range(edges.shape[1]):
        lower = jnp.where(has_lower, edges[0, group], 0.0)
        upper = jnp.where(has_upper, edges[1, group], 0.0)
        lane = lane_index(lower.shape)
        x = jnp.where(jnp.bitwise_and(lane, SLOT - 1) < HALO, upper, lower)
        keep = edge_mask(lane)
        for e in range(PER):
            at = tile(base + group * PER + e)
            grad[at] = grad[at] + jnp.where(keep, roll(x, (-HALO - SLOT * e) % LANES), 0.0)


def kernel(
    dims, sizes,
    inc_h, dep_h, weight_h, olon_h, olat_h, flon_h, flat_h, coup_h,
    tl, grad,
    wide, dep, weight, olon, olat, flon, flat, coup,
    edge_out, edge_in, e_source, e_olon, e_olat, e_flon, e_flat, e_lonw, e_latw, e_z,
    low, high, from_left, from_right, back_out, back_in, corner_left, corner_right,
    lonw, latw, t_lonw, t_latw, prime, ratio, inverse, z,
    load_sem, send, recv,
):
    fields, levels = dims
    pairs = fields // PAIR
    per_pair = PAIR * levels
    at = neighbours(sizes)
    band, bands = lax.axis_index("lat"), sizes[0]
    has_lower = band > 0
    has_upper = band < bands - 1
    numbers = iter(range(send.shape[0]))

    copies = [
        (olon_h, olon), (olat_h, olat), (flon_h, flon), (flat_h, flat),
        (inc_h, wide.at[:, 8:24]), (coup_h, coup), (dep_h, dep), (weight_h, weight),
    ]
    spare = olon.shape[0] - levels * 16
    for src, dst in copies[:4]:
        copies.append((src.at[0:spare], dst.at[levels * 16 : levels * 16 + spare]))
    copies[:4] = [(src, dst.at[0 : levels * 16]) for src, dst in copies[:4]]
    loads = [pltpu.make_async_copy(src, dst, load_sem.at[i]) for i, (src, dst) in enumerate(copies)]
    for load in loads:
        load.start()

    def launch(src, dst, device):
        copy = remote(src, dst, send, recv, next(numbers), device)
        copy.start()
        return copy

    def launch_lat(src, dst):
        down = remote(src, dst.at[1], send, recv, next(numbers), at(-1, 0))
        up = remote(src, dst.at[0], send, recv, next(numbers), at(1, 0))
        pl.when(has_lower)(down.start)
        pl.when(has_upper)(up.start)
        return down, up

    def finish_lat(copies):
        down, up = copies
        pl.when(has_lower)(down.wait_send)
        pl.when(has_upper)(down.wait_recv)
        pl.when(has_upper)(up.wait_send)
        pl.when(has_lower)(up.wait_recv)

    meet = greet([at(-1, 0), at(1, 0), at(0, -1), at(0, 1)])
    loads[4].wait()
    for pair in range(pairs):
        base = pair * per_pair
        pack_edges(lambda n, base=base: wide[base + n, 8:24], edge_out.at[pair])
    for load in (*loads[:4], *loads[8:]):
        load.wait()
    packed = (e_olon, e_olat, e_flon, e_flat)
    for src, dst in zip((olon, olat, flon, flat), packed):
        pack_edges(lambda n, src=src: src[pl.ds(n % levels * 16, 16)], dst)
    meet()
    edges = [launch_lat(edge_out.at[pair], edge_in.at[pair]) for pair in range(pairs)]
    around = []
    for pair in range(pairs):
        part = pl.ds(pair * per_pair, per_pair)
        around.append([
            launch(inc_h.at[part, 0 : HALO - 1], wide.at[part, 24 : 23 + HALO], at(0, -1)),
            launch(inc_h.at[part, 16 - HALO : 16], wide.at[part, 8 - HALO : 8], at(0, 1)),
        ])

    def launch_corners(src, left, right, rows):
        return [launch(src.at[:, of], dst.at[:, to], device)
                for of, dst, to, device in zip(rows[0::2], (left, right), rows[1::2], (at(0, -1), at(0, 1)))]

    store_across(levels, t_lonw, weights, olon, flon)
    store_across(levels, t_latw, lat_weights, olat, flat)

    @pl.loop(0, levels)
    def _(k):
        store_weights(lonw, k, weights(olon[tile(k)], flon[tile(k)]))
        store_weights(latw, k, lat_weights(olat[tile(k)], flat[tile(k)]))

    @pl.loop(0, e_olon.shape[0])
    def _(group):
        store_weights(e_lonw, group, weights(e_olon[group], e_flon[group]))
        store_weights(e_latw, group, edge_weights(e_olat[group], e_flat[group]))
        e_z[group] = jnp.zeros((TALL, LANES), jnp.float32)

    @pl.loop(0, fields * levels)
    def _(n):
        z[pl.ds(n * TALL, 8)] = jnp.zeros((8, LANES), jnp.float32)
        z[pl.ds(n * TALL + 24, 8)] = jnp.zeros((8, LANES), jnp.float32)
        grad[tile(n)] = wide[n, 8:24]

    inner = []
    for pair in range(pairs):
        finish_lat(edges[pair])
        source = e_source.at[pair]
        merge_edges(band, bands, edge_in.at[pair], source)
        rows = (pl.ds(8, HALO - 1), pl.ds(24, HALO - 1), pl.ds(24 - HALO, HALO), pl.ds(8 - HALO, HALO))
        inner.append(launch_corners(source, source, source, rows))

    advect(dims, range(fields), True, UNROLL, wide, olon, olat, flon, flat, prime)
    loads[5].wait()
    factor(dims, coup, ratio, inverse)
    for load in loads[6:8]:
        load.wait()

    across, outer = [], []
    for pair in range(pairs):
        base = pair * per_pair
        for copy in around[pair]:
            copy.wait()
        members = range(pair * PAIR, pair * PAIR + PAIR)
        advect(dims, members, False, 2 * UNROLL, wide, olon, olat, flon, flat, prime)
        for copy in inner[pair]:
            copy.wait()
        advect_edges(base, e_source.at[pair], packed, prime)
        solve(dims, pair * PAIR, prime, ratio, inverse, coup, dep, weight, tl, z)
        pack_edges(lambda n, base=base: z[pl.ds((base + n) * TALL + 8, 16)], e_z)
        spread_edges(e_z, e_lonw, e_latw, back_out.at[pair])
        rows = (pl.ds(8 - HALO, HALO), pl.ds(24 - HALO, HALO), pl.ds(24, HALO - 1), pl.ds(8, HALO - 1))
        outer.append(launch_corners(back_out.at[pair], corner_right.at[pair], corner_left.at[pair], rows))
        spread_lon(dims, base, z, t_lonw, t_latw, low.at[pair], high.at[pair])
        across.append([
            launch(low.at[pair], from_right.at[pair], at(0, -1)),
            launch(high.at[pair], from_left.at[pair], at(0, 1)),
        ])

    returned = []

    def pass_back(pair):
        for copy in outer[pair]:
            copy.wait()
        add_corners(corner_left.at[pair], corner_right.at[pair], back_out.at[pair])
        returned.append(launch_lat(back_out.at[pair, :, 8:24], back_in.at[pair]))

    def close(pair):
        base = pair * per_pair
        for copy in across[pair]:
            copy.wait()
        gather_lon(base, from_left.at[pair], from_right.at[pair], grad)
        finish_lat(returned[pair])
        finish(base, band, bands, back_in.at[pair], grad)

    for pair in range(pairs):
        base = pair * per_pair
        if pair == 0:
            pass_back(pair)
        else:
            close(pair)
        collect(dims, base, z, lonw, latw, grad)
        if pair == 0:
            for later in range(1, pairs):
                pass_back(later)
            close(pair)


def place(a, b, a_h, b_h, sem):
    moves = [pltpu.make_async_copy(a, a_h, sem.at[0]), pltpu.make_async_copy(b, b_h, sem.at[1])]
    for move in moves:
        move.start()
    for move in moves:
        move.wait()


def shards(sizes, increment, obs_dep, obs_weight, dep_lon, dep_lat, frac_lon, frac_lat, coupling):
    fields, levels, rows, cols = increment.shape
    count = fields * levels
    pairs = fields // PAIR
    groups = PAIR * levels // PER
    spare = max(g * PER % levels for g in range(groups)) + PER - levels
    dims = (fields, levels)

    def vmem(*s, dtype=jnp.float32):
        return pltpu.VMEM(s, dtype)

    def flat2(x):
        return x.reshape(-1, cols)

    def flat3(x):
        return x.reshape(-1, rows, cols)

    field = vmem(count, rows, cols)
    level = vmem((levels + spare) * rows, cols)
    index = vmem((levels + spare) * rows, cols, dtype=jnp.int32)
    edge = vmem(groups, rows, cols)
    edge_index = vmem(groups, rows, cols, dtype=jnp.int32)
    edges = vmem(pairs, groups, TALL, cols)
    sides = vmem(pairs, 2, groups, rows, cols)
    low = vmem(pairs, groups, HALO, 8, cols)
    high = vmem(pairs, groups, HALO - 1, 8, cols)
    steps = len(SHIFTS)
    main_w = vmem(steps, levels * TALL, cols)
    edge_w = vmem(steps, groups * TALL, cols)
    outer_w = vmem(steps, groups, len(OUTER), PER, cols)
    copies = pairs * 12
    tl, grad = pl.pallas_call(
        functools.partial(kernel, dims, sizes),
        out_shape=(
            jax.ShapeDtypeStruct((count, rows, cols), jnp.float32),
            jax.ShapeDtypeStruct((count * rows, cols), jnp.float32),
        ),
        in_specs=[ANY] * 8,
        out_specs=(WITHIN, WITHIN),
        scratch_shapes=[
            vmem(count, TALL, cols), field, field, index, index, level, level,
            vmem(fields * (levels - 1), rows, cols),
            vmem(pairs, groups, rows, cols), sides, edges,
            edge_index, edge_index, edge, edge, edge_w, vmem(HALO, groups * TALL, cols), vmem(groups, TALL, cols),
            low, high, high, low, edges, sides, edges, edges,
            main_w, main_w, outer_w, outer_w, field, field, field, vmem(count * TALL, cols),
            pltpu.SemaphoreType.DMA((12,)),
            pltpu.SemaphoreType.DMA((copies,)),
            pltpu.SemaphoreType.DMA((copies,)),
        ],
        compiler_params=pltpu.CompilerParams(
            collective_id=0, has_side_effects=True, vmem_limit_bytes=LIMIT
        ),
    )(
        *(pltpu.with_memory_space_constraint(x, pltpu.HBM) for x in (
            flat3(increment), flat3(obs_dep), flat3(obs_weight), flat2(dep_lon), flat2(dep_lat),
            flat2(frac_lon), flat2(frac_lat), flat3(coupling),
        ))
    )
    tl, grad = pl.pallas_call(
        place,
        out_shape=tuple(jax.ShapeDtypeStruct(x.shape, x.dtype) for x in (tl, grad)),
        in_specs=[WITHIN] * 2,
        out_specs=(ANY, ANY),
        scratch_shapes=[pltpu.SemaphoreType.DMA((2,))],
        compiler_params=pltpu.CompilerParams(vmem_limit_bytes=4 * 1024 * 1024),
    )(tl, grad)
    return tl.reshape(increment.shape), grad.reshape(increment.shape)


def solution(mesh):
    sizes = (mesh.shape["lat"], mesh.shape["lon"])
    wide = P(None, None, "lon", "lat")
    level = P(None, "lon", "lat")
    return jax.shard_map(
        functools.partial(shards, sizes),
        mesh=mesh,
        in_specs=(wide, wide, wide, level, level, level, level, wide),
        out_specs=(wide, wide),
        check_vma=False,
    )
```

```python
import functools

import jax
import jax.numpy as jnp
from jax import lax
from jax.experimental import pallas as pl
from jax.experimental.pallas import tpu as pltpu
from jax.sharding import PartitionSpec as P

HALO = 6
SHIFTS = tuple(range(1 - HALO, HALO + 1))
LANES = 128
SLOT = 16
PER = LANES // SLOT
TALL = 32
PAIR = 2
OUTER = (*range(HALO), *range(17 - HALO, 16))
UNROLL = 2
MESH = pl.DeviceIdType.MESH
ANY = pl.BlockSpec(memory_space=pl.ANY)
WITHIN = pl.BlockSpec(memory_space=pltpu.VMEM)
LIMIT = 44 * 1024 * 1024


def lane_index(shape):
    return lax.broadcasted_iota(jnp.int32, shape, len(shape) - 1)


def roll(x, shift):
    return pltpu.roll(x, shift, x.ndim - 1)


def neighbours(sizes):
    lat, lon = lax.axis_index("lat"), lax.axis_index("lon")

    def at(dy, dx):
        return {
            "lat": lax.rem(lat + dy + sizes[0], sizes[0]),
            "lon": lax.rem(lon + dx + sizes[1], sizes[1]),
        }

    return at


def greet(devices):
    barrier = pltpu.get_barrier_semaphore()
    for device in devices:
        pl.semaphore_signal(barrier, inc=1, device_id=device, device_id_type=MESH)
    return lambda: pl.semaphore_wait(barrier, len(devices))


def remote(src, dst, send, recv, number, device):
    return pltpu.make_async_remote_copy(
        src_ref=src,
        dst_ref=dst,
        send_sem=send.at[number],
        recv_sem=recv.at[number],
        device_id=device,
        device_id_type=MESH,
    )


def tile(n, height=16):
    return pl.ds(pl.multiple_of(n * height, 8), height)


def pick(base, row, height):
    return pl.ds(base * height + row, 8, stride=height)


def edge_mask(lane):
    return (lane < HALO) | (lane >= LANES - HALO)


def pack_edges(load, dst):
    for group in range(dst.shape[0]):
        total = None
        for e in range(PER):
            x = load(group * PER + e)
            x = jnp.where(edge_mask(lane_index(x.shape)), x, jnp.zeros_like(x))
            x = roll(x, (HALO + SLOT * e) % LANES)
            total = x if total is None else total + x
        if dst.shape[1] == TALL:
            dst[group, 8:24] = total
        else:
            dst[group] = total


def weights(offset, frac):
    rest = 1.0 - frac
    before = None
    for total in SHIFTS:
        here = offset == total
        second = 0.0 if before is None else jnp.where(before, frac, 0.0)
        yield total, jnp.where(here, rest, second)
        before = here


def lat_weights(offset, frac):
    lane = lane_index(frac.shape)
    for n, w in weights(offset, frac):
        yield n, w if n == 0 else jnp.where((lane >= n) if n > 0 else (lane < LANES + n), w, 0.0)


def edge_weights(offset, frac):
    high = jnp.bitwise_and(lane_index(frac.shape), SLOT - 1) < HALO
    by = dict(weights(offset, frac))
    for n in range(1, HALO + 1):
        yield n, jnp.where(high, by.get(-n, 0.0), by[n])


def store_weights(dst, k, values):
    blank = jnp.zeros((8, LANES), jnp.float32)
    for pos, (_, w) in enumerate(values):
        dst[pos, pl.ds(k * TALL, 8)] = blank
        dst[pos, pl.ds(k * TALL + 8, 16)] = w
        dst[pos, pl.ds(k * TALL + 24, 8)] = blank


def store_across(levels, dst, kind, offset, frac):
    @pl.loop(0, dst.shape[1])
    def _(group):
        level = lax.rem(group * PER, levels)
        for i, j in enumerate(OUTER):
            values = kind(offset[pick(level, j, 16)], frac[pick(level, j, 16)])
            for pos, (_, w) in enumerate(values):
                dst[pos, group, i] = w


def factor(dims, coup, ratio, inverse):
    fields, levels = dims
    previous = [None] * fields
    for k in range(levels):
        for f in range(fields):
            at, c = f * levels + k, f * (levels - 1) + k
            denom = 1.0
            if k > 0:
                below = coup[c - 1]
                denom = denom + below
            if k < levels - 1:
                above = coup[c]
                denom = denom + above
            if k > 0:
                denom = denom - below * previous[f]
            inv = 1.0 / denom
            inverse[at] = inv
            if k < levels - 1:
                previous[f] = above * inv
                ratio[at] = previous[f]


def split_lon(step, part):
    evens, odds = jnp.bitwise_and(step + 1, -2), jnp.bitwise_or(step, 1)
    is_even = step == evens
    return (evens, odds), (jnp.where(is_even, 1.0 - part, part), jnp.where(is_even, part, 1.0 - part))


def interpolate(loads, half, index, lat_w, chosen, lon_w, shifts):
    found = {}
    masks = {total: chosen[total % 2] == total for total in shifts}
    for q in range(2):
        for total in shifts:
            near = 8 + 8 * half - total
            for m, load in enumerate(loads):
                x = jnp.take_along_axis(load(near), index[q], axis=1)
                key = (m, total % 2, q)
                found[key] = jnp.where(masks[total], x, found.get(key, 0.0))
    out = []
    for m in range(len(loads)):
        parts = [
            lon_w[o] * (lat_w[0] * found[m, o, 0] + lat_w[1] * found[m, o, 1]) for o in range(2)
        ]
        out.append(parts[0] + parts[1])
    return out


def advect(dims, numbers, own, unroll, wide, olon, olat, flon, flat, prime):
    levels = dims[1]
    lane = lane_index((8, LANES))

    @pl.loop(0, levels // unroll)
    def _(block):
        for k in [block * unroll + i for i in range(unroll)]:
            for half in range(2):
                rows = pl.ds(8 * half, 8)
                here = pl.ds(k * 16 + 8 * half, 8)
                raw = [lane - olat[here] - q for q in range(2)]
                index = [jnp.bitwise_and(x, LANES - 1) for x in raw]
                one = flat[here]
                lat_w = [
                    jnp.where((x >= 0) & (x < LANES), w, 0.0) for x, w in zip(raw, (1.0 - one, one))
                ]
                chosen, lon_w = split_lon(olon[here], flon[here])
                shifts = [n for n in SHIFTS if own == (n <= 0 if half == 0 else n >= 0)]
                loads = [lambda near, f=f, k=k: wide[f * levels + k, pl.ds(near, 8)] for f in numbers]
                for f, x in zip(numbers, interpolate(loads, half, index, lat_w, chosen, lon_w, shifts)):
                    prime[f * levels + k, rows] = x if own else prime[f * levels + k, rows] + x


def merge_edges(band, bands, edges, source):
    has_lower = band > 0
    has_upper = band < bands - 1

    @pl.loop(0, edges.shape[1])
    def _(group):
        slot = jnp.bitwise_and(lane_index((16, LANES)), SLOT - 1)
        lower = jnp.where(has_lower, edges[0, group], 0.0)
        upper = jnp.where(has_upper, edges[1, group], 0.0)
        source[group, 8:24] = jnp.where(slot < HALO, lower, upper)


def advect_edges(base, source, packed, prime):
    e_olon, e_olat, e_flon, e_flat = packed
    lane = lane_index((8, LANES))
    slot = jnp.bitwise_and(lane, SLOT - 1)
    keep = edge_mask(lane)
    for group, half in [(group, half) for group in range(source.shape[0]) for half in range(2)]:
        rows = pl.ds(8 * half, 8)
        olat = e_olat[group, rows]
        one = e_flat[group, rows]
        index, lat_w = [], []
        for q, w in enumerate((1.0 - one, one)):
            near = slot - olat - q
            valid = ((slot < HALO) & (near >= HALO)) | (
                (slot >= HALO) & (slot < 2 * HALO) & (near < HALO)
            )
            lat_w.append(jnp.where(valid, w, 0.0))
            index.append(jnp.bitwise_and(lane - olat - q, LANES - 1))
        chosen, lon_w = split_lon(e_olon[group, rows], e_flon[group, rows])
        loads = [lambda near, group=group: source[group, pl.ds(near, 8)]]
        x = interpolate(loads, half, index, lat_w, chosen, lon_w, SHIFTS)[0]
        for e in range(PER):
            at = base + group * PER + e
            prime[at, rows] = prime[at, rows] + jnp.where(
                keep, roll(x, (-HALO - SLOT * e) % LANES), 0.0
            )


def solve(dims, first_field, prime, ratio, inverse, coup, dep, weight, tl, z):
    fields, levels = dims
    members = range(first_field, first_field + PAIR)
    x = {}
    for k in range(levels):
        for f in members:
            at = f * levels + k
            value = prime[at]
            if k > 0:
                value = value + coup[f * (levels - 1) + k - 1] * x[f]
            x[f] = value * inverse[at]
            prime[at] = x[f]
    for k in range(levels - 1, -1, -1):
        for f in members:
            at = f * levels + k
            x[f] = prime[at] if k == levels - 1 else prime[at] + ratio[at] * x[f]
            tl[at] = x[f]
    for k in range(levels):
        for f in members:
            at = f * levels + k
            forcing = weight[at] * (tl[at] - dep[at])
            if k > 0:
                forcing = forcing + coup[f * (levels - 1) + k - 1] * x[f]
            x[f] = forcing * inverse[at]
            prime[at] = x[f]
    for k in range(levels - 1, -1, -1):
        for f in members:
            at = f * levels + k
            x[f] = prime[at] if k == levels - 1 else prime[at] + ratio[at] * x[f]
            z[pl.ds(at * TALL + 8, 16)] = x[f]


def shifted(x, n):
    return x if n == 0 else roll(x, (-n) % LANES)


def spread_lon(dims, base, z, lonw, latw, low, high):
    @pl.loop(0, low.shape[0])
    def _(group):
        number = base + group * PER
        for out, targets, sources in (
            (low, range(-HALO, 0), range(HALO)),
            (high, range(16, 15 + HALO), range(17 - HALO, 16)),
        ):
            scaled = {}
            for j in sources:
                x = z[pick(number, 8 + j, TALL)]
                for a in targets:
                    if j - a in SHIFTS:
                        scaled[a, j] = x * lonw[SHIFTS.index(j - a), group, OUTER.index(j)]
            total = {}
            for pos, n in enumerate(SHIFTS):
                w = {j: latw[pos, group, OUTER.index(j)] for j in sources}
                for a in targets:
                    terms = [w[j] * scaled[a, j] for j in sources if (a, j) in scaled]
                    x = shifted(functools.reduce(jnp.add, terms), n)
                    total[a] = total[a] + x if a in total else x
            for e, a in enumerate(targets):
                out[group, e] = total[a]


def spread_edges(z, lonw, latw, result):
    slot = jnp.bitwise_and(lane_index((8, LANES)), SLOT - 1)

    @pl.loop(0, result.shape[0])
    def _(group):
        for part, steps in enumerate((range(1, HALO + 1), SHIFTS, SHIFTS, range(1 - HALO, 0))):
            sums = {}
            for r in steps:
                near = 8 * part + r
                scaled = lonw[SHIFTS.index(r), pl.ds(group * TALL + near, 8)] * z[group, pl.ds(near, 8)]
                for n in range(1, HALO + 1):
                    term = latw[n - 1, pl.ds(group * TALL + near, 8)] * scaled
                    sums[n] = sums[n] + term if n in sums else term
            total = None
            for n, x in sums.items():
                down = jnp.where((slot >= HALO - n) & (slot < HALO), shifted(x, n), 0.0)
                up = jnp.where((slot >= HALO) & (slot < HALO + n), shifted(x, -n), 0.0)
                total = down + up if total is None else total + (down + up)
            result[group, 8 * part : 8 * part + 8] = total


def add_corners(left, right, result):
    @pl.loop(0, result.shape[0])
    def _(group):
        row = lax.broadcasted_iota(jnp.int32, (8, LANES), 0)
        result[group, 8:16] = result[group, 8:16] + jnp.where(row < HALO - 1, left[group, 8:16], 0.0)
        result[group, 16:24] = result[group, 16:24] + jnp.where(row >= 8 - HALO, right[group, 16:24], 0.0)


def gather_lon(base, from_left, from_right, grad):
    @pl.loop(0, from_left.shape[0])
    def _(group):
        number = group * PER
        for side, first in ((from_right, 16 - HALO), (from_left, 0)):
            for e in range(side.shape[1]):
                at = pick(base + number, first + e, 16)
                grad[at] = grad[at] + side[group, e]


def collect(dims, base, z, lonw, latw, grad):
    levels = dims[1]

    @pl.loop(0, levels)
    def _(k):
        for half in range(2):
            sums = {}
            for lon_pos, lon_total in enumerate(SHIFTS):
                near = 8 + 8 * half + lon_total
                scale = lonw[lon_pos, pl.ds(k * TALL + near, 8)]
                scaled = [scale * z[pl.ds((base + f * levels + k) * TALL + near, 8)] for f in range(PAIR)]
                for pos in range(len(SHIFTS)):
                    w = latw[pos, pl.ds(k * TALL + near, 8)]
                    for f in range(PAIR):
                        term = w * scaled[f]
                        sums[f, pos] = term if lon_pos == 0 else sums[f, pos] + term
            for f in range(PAIR):
                at = pl.ds((base + f * levels + k) * 16 + 8 * half, 8)
                total = grad[at]
                for pos, n in enumerate(SHIFTS):
                    total = total + shifted(sums[f, pos], n)
                grad[at] = total


def finish(base, band, bands, edges, grad):
    has_lower = band > 0
    has_upper = band < bands - 1

    for group in range(edges.shape[1]):
        lower = jnp.where(has_lower, edges[0, group], 0.0)
        upper = jnp.where(has_upper, edges[1, group], 0.0)
        lane = lane_index(lower.shape)
        x = jnp.where(jnp.bitwise_and(lane, SLOT - 1) < HALO, upper, lower)
        keep = edge_mask(lane)
        for e in range(PER):
            at = tile(base + group * PER + e)
            grad[at] = grad[at] + jnp.where(keep, roll(x, (-HALO - SLOT * e) % LANES), 0.0)


def kernel(
    dims, sizes,
    inc_h, dep_h, weight_h, olon_h, olat_h, flon_h, flat_h, coup_h,
    tl, grad,
    wide, dep, weight, olon, olat, flon, flat, coup,
    edge_out, edge_in, e_source, e_olon, e_olat, e_flon, e_flat, e_lonw, e_latw, e_z,
    low, high, from_left, from_right, back_out, back_in, corner_left, corner_right,
    lonw, latw, t_lonw, t_latw, prime, ratio, inverse, z,
    load_sem, send, recv,
):
    fields, levels = dims
    pairs = fields // PAIR
    per_pair = PAIR * levels
    at = neighbours(sizes)
    band, bands = lax.axis_index("lat"), sizes[0]
    has_lower = band > 0
    has_upper = band < bands - 1
    numbers = iter(range(send.shape[0]))

    copies = [
        (olon_h, olon), (olat_h, olat), (flon_h, flon), (flat_h, flat),
        (inc_h, wide.at[:, 8:24]), (coup_h, coup), (dep_h, dep), (weight_h, weight),
    ]
    spare = olon.shape[0] - levels * 16
    for src, dst in copies[:4]:
        copies.append((src.at[0:spare], dst.at[levels * 16 : levels * 16 + spare]))
    copies[:4] = [(src, dst.at[0 : levels * 16]) for src, dst in copies[:4]]
    loads = [pltpu.make_async_copy(src, dst, load_sem.at[i]) for i, (src, dst) in enumerate(copies)]
    for load in loads:
        load.start()

    def launch(src, dst, device):
        copy = remote(src, dst, send, recv, next(numbers), device)
        copy.start()
        return copy

    def launch_lat(src, dst):
        down = remote(src, dst.at[1], send, recv, next(numbers), at(-1, 0))
        up = remote(src, dst.at[0], send, recv, next(numbers), at(1, 0))
        pl.when(has_lower)(down.start)
        pl.when(has_upper)(up.start)
        return down, up

    def finish_lat(copies):
        down, up = copies
        pl.when(has_lower)(down.wait_send)
        pl.when(has_upper)(down.wait_recv)
        pl.when(has_upper)(up.wait_send)
        pl.when(has_lower)(up.wait_recv)

    meet = greet([at(-1, 0), at(1, 0), at(0, -1), at(0, 1)])
    loads[4].wait()
    for pair in range(pairs):
        base = pair * per_pair
        pack_edges(lambda n, base=base: wide[base + n, 8:24], edge_out.at[pair])
    for load in (*loads[:4], *loads[8:]):
        load.wait()
    packed = (e_olon, e_olat, e_flon, e_flat)
    for src, dst in zip((olon, olat, flon, flat), packed):
        pack_edges(lambda n, src=src: src[pl.ds(n % levels * 16, 16)], dst)
    meet()
    edges = [launch_lat(edge_out.at[pair], edge_in.at[pair]) for pair in range(pairs)]
    around = []
    for pair in range(pairs):
        part = pl.ds(pair * per_pair, per_pair)
        around.append([
            launch(inc_h.at[part, 0 : HALO - 1], wide.at[part, 24 : 23 + HALO], at(0, -1)),
            launch(inc_h.at[part, 16 - HALO : 16], wide.at[part, 8 - HALO : 8], at(0, 1)),
        ])

    def launch_corners(src, left, right, rows):
        return [launch(src.at[:, of], dst.at[:, to], device)
                for of, dst, to, device in zip(rows[0::2], (left, right), rows[1::2], (at(0, -1), at(0, 1)))]

    store_across(levels, t_lonw, weights, olon, flon)
    store_across(levels, t_latw, lat_weights, olat, flat)

    @pl.loop(0, levels)
    def _(k):
        store_weights(lonw, k, weights(olon[tile(k)], flon[tile(k)]))
        store_weights(latw, k, lat_weights(olat[tile(k)], flat[tile(k)]))

    @pl.loop(0, e_olon.shape[0])
    def _(group):
        store_weights(e_lonw, group, weights(e_olon[group], e_flon[group]))
        store_weights(e_latw, group, edge_weights(e_olat[group], e_flat[group]))
        e_z[group] = jnp.zeros((TALL, LANES), jnp.float32)

    @pl.loop(0, fields * levels)
    def _(n):
        z[pl.ds(n * TALL, 8)] = jnp.zeros((8, LANES), jnp.float32)
        z[pl.ds(n * TALL + 24, 8)] = jnp.zeros((8, LANES), jnp.float32)
        grad[tile(n)] = wide[n, 8:24]

    inner = []
    for pair in range(pairs):
        finish_lat(edges[pair])
        source = e_source.at[pair]
        merge_edges(band, bands, edge_in.at[pair], source)
        rows = (pl.ds(8, HALO - 1), pl.ds(24, HALO - 1), pl.ds(24 - HALO, HALO), pl.ds(8 - HALO, HALO))
        inner.append(launch_corners(source, source, source, rows))

    advect(dims, range(fields), True, UNROLL, wide, olon, olat, flon, flat, prime)
    loads[5].wait()
    factor(dims, coup, ratio, inverse)
    for load in loads[6:8]:
        load.wait()

    across, outer = [], []
    for pair in range(pairs):
        base = pair * per_pair
        for copy in around[pair]:
            copy.wait()
        members = range(pair * PAIR, pair * PAIR + PAIR)
        advect(dims, members, False, 2 * UNROLL, wide, olon, olat, flon, flat, prime)
        for copy in inner[pair]:
            copy.wait()
        advect_edges(base, e_source.at[pair], packed, prime)
        solve(dims, pair * PAIR, prime, ratio, inverse, coup, dep, weight, tl, z)
        pack_edges(lambda n, base=base: z[pl.ds((base + n) * TALL + 8, 16)], e_z)
        spread_edges(e_z, e_lonw, e_latw, back_out.at[pair])
        rows = (pl.ds(8 - HALO, HALO), pl.ds(24 - HALO, HALO), pl.ds(24, HALO - 1), pl.ds(8, HALO - 1))
        outer.append(launch_corners(back_out.at[pair], corner_right.at[pair], corner_left.at[pair], rows))
        spread_lon(dims, base, z, t_lonw, t_latw, low.at[pair], high.at[pair])
        across.append([
            launch(low.at[pair], from_right.at[pair], at(0, -1)),
            launch(high.at[pair], from_left.at[pair], at(0, 1)),
        ])

    returned = []

    def pass_back(pair):
        for copy in outer[pair]:
            copy.wait()
        add_corners(corner_left.at[pair], corner_right.at[pair], back_out.at[pair])
        returned.append(launch_lat(back_out.at[pair, :, 8:24], back_in.at[pair]))

    def close(pair):
        base = pair * per_pair
        for copy in across[pair]:
            copy.wait()
        gather_lon(base, from_left.at[pair], from_right.at[pair], grad)
        finish_lat(returned[pair])
        finish(base, band, bands, back_in.at[pair], grad)

    pass_back(0)
    for pair in range(pairs):
        collect(dims, pair * per_pair, z, lonw, latw, grad)
        if pair + 1 < pairs:
            pass_back(pair + 1)
        close(pair)


def place(a, b, a_h, b_h, sem):
    moves = [pltpu.make_async_copy(a, a_h, sem.at[0]), pltpu.make_async_copy(b, b_h, sem.at[1])]
    for move in moves:
        move.start()
    for move in moves:
        move.wait()


def shards(sizes, increment, obs_dep, obs_weight, dep_lon, dep_lat, frac_lon, frac_lat, coupling):
    fields, levels, rows, cols = increment.shape
    count = fields * levels
    pairs = fields // PAIR
    groups = PAIR * levels // PER
    spare = max(g * PER % levels for g in range(groups)) + PER - levels
    dims = (fields, levels)

    def vmem(*s, dtype=jnp.float32):
        return pltpu.VMEM(s, dtype)

    def flat2(x):
        return x.reshape(-1, cols)

    def flat3(x):
        return x.reshape(-1, rows, cols)

    field = vmem(count, rows, cols)
    level = vmem((levels + spare) * rows, cols)
    index = vmem((levels + spare) * rows, cols, dtype=jnp.int32)
    edge = vmem(groups, rows, cols)
    edge_index = vmem(groups, rows, cols, dtype=jnp.int32)
    edges = vmem(pairs, groups, TALL, cols)
    sides = vmem(pairs, 2, groups, rows, cols)
    low = vmem(pairs, groups, HALO, 8, cols)
    high = vmem(pairs, groups, HALO - 1, 8, cols)
    steps = len(SHIFTS)
    main_w = vmem(steps, levels * TALL, cols)
    edge_w = vmem(steps, groups * TALL, cols)
    outer_w = vmem(steps, groups, len(OUTER), PER, cols)
    copies = pairs * 12
    tl, grad = pl.pallas_call(
        functools.partial(kernel, dims, sizes),
        out_shape=(
            jax.ShapeDtypeStruct((count, rows, cols), jnp.float32),
            jax.ShapeDtypeStruct((count * rows, cols), jnp.float32),
        ),
        in_specs=[ANY] * 8,
        out_specs=(WITHIN, WITHIN),
        scratch_shapes=[
            vmem(count, TALL, cols), field, field, index, index, level, level,
            vmem(fields * (levels - 1), rows, cols),
            vmem(pairs, groups, rows, cols), sides, edges,
            edge_index, edge_index, edge, edge, edge_w, vmem(HALO, groups * TALL, cols), vmem(groups, TALL, cols),
            low, high, high, low, edges, sides, edges, edges,
            main_w, main_w, outer_w, outer_w, field, field, field, vmem(count * TALL, cols),
            pltpu.SemaphoreType.DMA((12,)),
            pltpu.SemaphoreType.DMA((copies,)),
            pltpu.SemaphoreType.DMA((copies,)),
        ],
        compiler_params=pltpu.CompilerParams(
            collective_id=0, has_side_effects=True, vmem_limit_bytes=LIMIT
        ),
    )(
        *(pltpu.with_memory_space_constraint(x, pltpu.HBM) for x in (
            flat3(increment), flat3(obs_dep), flat3(obs_weight), flat2(dep_lon), flat2(dep_lat),
            flat2(frac_lon), flat2(frac_lat), flat3(coupling),
        ))
    )
    tl, grad = pl.pallas_call(
        place,
        out_shape=tuple(jax.ShapeDtypeStruct(x.shape, x.dtype) for x in (tl, grad)),
        in_specs=[WITHIN] * 2,
        out_specs=(ANY, ANY),
        scratch_shapes=[pltpu.SemaphoreType.DMA((2,))],
        compiler_params=pltpu.CompilerParams(vmem_limit_bytes=4 * 1024 * 1024),
    )(tl, grad)
    return tl.reshape(increment.shape), grad.reshape(increment.shape)


def solution(mesh):
    sizes = (mesh.shape["lat"], mesh.shape["lon"])
    wide = P(None, None, "lon", "lat")
    level = P(None, "lon", "lat")
    return jax.shard_map(
        functools.partial(shards, sizes),
        mesh=mesh,
        in_specs=(wide, wide, wide, level, level, level, level, wide),
        out_specs=(wide, wide),
        check_vma=False,
    )
```

```python
import functools

import jax
import jax.numpy as jnp
from jax import lax
from jax.experimental import pallas as pl
from jax.experimental.pallas import tpu as pltpu
from jax.sharding import PartitionSpec as P

HALO = 6
SHIFTS = tuple(range(1 - HALO, HALO + 1))
LANES = 128
SLOT = 16
PER = LANES // SLOT
TALL = 32
PAIR = 2
OUTER = (*range(HALO), *range(17 - HALO, 16))
UNROLL = 2
MESH = pl.DeviceIdType.MESH
ANY = pl.BlockSpec(memory_space=pl.ANY)
WITHIN = pl.BlockSpec(memory_space=pltpu.VMEM)
LIMIT = 44 * 1024 * 1024


def lane_index(shape):
    return lax.broadcasted_iota(jnp.int32, shape, len(shape) - 1)


def roll(x, shift):
    return pltpu.roll(x, shift, x.ndim - 1)


def neighbours(sizes):
    lat, lon = lax.axis_index("lat"), lax.axis_index("lon")

    def at(dy, dx):
        return {
            "lat": lax.rem(lat + dy + sizes[0], sizes[0]),
            "lon": lax.rem(lon + dx + sizes[1], sizes[1]),
        }

    return at


def greet(devices):
    barrier = pltpu.get_barrier_semaphore()
    for device in devices:
        pl.semaphore_signal(barrier, inc=1, device_id=device, device_id_type=MESH)
    return lambda: pl.semaphore_wait(barrier, len(devices))


def remote(src, dst, send, recv, number, device):
    return pltpu.make_async_remote_copy(
        src_ref=src,
        dst_ref=dst,
        send_sem=send.at[number],
        recv_sem=recv.at[number],
        device_id=device,
        device_id_type=MESH,
    )


def tile(n, height=16):
    return pl.ds(pl.multiple_of(n * height, 8), height)


def pick(base, row, height):
    return pl.ds(base * height + row, 8, stride=height)


def edge_mask(lane):
    return (lane < HALO) | (lane >= LANES - HALO)


def pack_edges(load, dst):
    for group in range(dst.shape[0]):
        total = None
        for e in range(PER):
            x = load(group * PER + e)
            x = jnp.where(edge_mask(lane_index(x.shape)), x, jnp.zeros_like(x))
            x = roll(x, (HALO + SLOT * e) % LANES)
            total = x if total is None else total + x
        if dst.shape[1] == TALL:
            dst[group, 8:24] = total
        else:
            dst[group] = total


def weights(offset, frac):
    rest = 1.0 - frac
    before = None
    for total in SHIFTS:
        here = offset == total
        second = 0.0 if before is None else jnp.where(before, frac, 0.0)
        yield total, jnp.where(here, rest, second)
        before = here


def lat_weights(offset, frac):
    lane = lane_index(frac.shape)
    for n, w in weights(offset, frac):
        yield n, w if n == 0 else jnp.where((lane >= n) if n > 0 else (lane < LANES + n), w, 0.0)


def edge_weights(offset, frac):
    high = jnp.bitwise_and(lane_index(frac.shape), SLOT - 1) < HALO
    by = dict(weights(offset, frac))
    for n in range(1, HALO + 1):
        yield n, jnp.where(high, by.get(-n, 0.0), by[n])


def store_weights(dst, k, values):
    blank = jnp.zeros((8, LANES), jnp.float32)
    for pos, (_, w) in enumerate(values):
        dst[pos, pl.ds(k * TALL, 8)] = blank
        dst[pos, pl.ds(k * TALL + 8, 16)] = w
        dst[pos, pl.ds(k * TALL + 24, 8)] = blank


def store_across(levels, dst, kind, offset, frac):
    @pl.loop(0, dst.shape[1])
    def _(group):
        level = lax.rem(group * PER, levels)
        for i, j in enumerate(OUTER):
            values = kind(offset[pick(level, j, 16)], frac[pick(level, j, 16)])
            for pos, (_, w) in enumerate(values):
                dst[pos, group, i] = w


def factor(dims, coup, ratio, inverse):
    fields, levels = dims
    previous = [None] * fields
    for k in range(levels):
        for f in range(fields):
            at, c = f * levels + k, f * (levels - 1) + k
            denom = 1.0
            if k > 0:
                below = coup[c - 1]
                denom = denom + below
            if k < levels - 1:
                above = coup[c]
                denom = denom + above
            if k > 0:
                denom = denom - below * previous[f]
            inv = 1.0 / denom
            inverse[at] = inv
            if k < levels - 1:
                previous[f] = above * inv
                ratio[at] = previous[f]


def split_lon(step, part):
    evens, odds = jnp.bitwise_and(step + 1, -2), jnp.bitwise_or(step, 1)
    is_even = step == evens
    return (evens, odds), (jnp.where(is_even, 1.0 - part, part), jnp.where(is_even, part, 1.0 - part))


def interpolate(loads, half, index, lat_w, chosen, lon_w, shifts):
    found = {}
    masks = {total: chosen[total % 2] == total for total in shifts}
    for q in range(2):
        for total in shifts:
            near = 8 + 8 * half - total
            for m, load in enumerate(loads):
                x = jnp.take_along_axis(load(near), index[q], axis=1)
                key = (m, total % 2, q)
                found[key] = jnp.where(masks[total], x, found.get(key, 0.0))
    out = []
    for m in range(len(loads)):
        parts = [
            lon_w[o] * (lat_w[0] * found[m, o, 0] + lat_w[1] * found[m, o, 1]) for o in range(2)
        ]
        out.append(parts[0] + parts[1])
    return out


def advect(dims, numbers, own, unroll, wide, olon, olat, flon, flat, prime):
    levels = dims[1]
    lane = lane_index((8, LANES))

    @pl.loop(0, levels // unroll)
    def _(block):
        for k in [block * unroll + i for i in range(unroll)]:
            for half in range(2):
                rows = pl.ds(8 * half, 8)
                here = pl.ds(k * 16 + 8 * half, 8)
                raw = [lane - olat[here] - q for q in range(2)]
                index = [jnp.bitwise_and(x, LANES - 1) for x in raw]
                one = flat[here]
                lat_w = [
                    jnp.where((x >= 0) & (x < LANES), w, 0.0) for x, w in zip(raw, (1.0 - one, one))
                ]
                chosen, lon_w = split_lon(olon[here], flon[here])
                shifts = [n for n in SHIFTS if own == (n <= 0 if half == 0 else n >= 0)]
                loads = [lambda near, f=f, k=k: wide[f * levels + k, pl.ds(near, 8)] for f in numbers]
                for f, x in zip(numbers, interpolate(loads, half, index, lat_w, chosen, lon_w, shifts)):
                    prime[f * levels + k, rows] = x if own else prime[f * levels + k, rows] + x


def merge_edges(band, bands, edges, source):
    has_lower = band > 0
    has_upper = band < bands - 1

    @pl.loop(0, edges.shape[1])
    def _(group):
        slot = jnp.bitwise_and(lane_index((16, LANES)), SLOT - 1)
        lower = jnp.where(has_lower, edges[0, group], 0.0)
        upper = jnp.where(has_upper, edges[1, group], 0.0)
        source[group, 8:24] = jnp.where(slot < HALO, lower, upper)


def advect_edges(base, source, packed, prime):
    e_olon, e_olat, e_flon, e_flat = packed
    lane = lane_index((8, LANES))
    slot = jnp.bitwise_and(lane, SLOT - 1)
    keep = edge_mask(lane)
    for group, half in [(group, half) for group in range(source.shape[0]) for half in range(2)]:
        rows = pl.ds(8 * half, 8)
        olat = e_olat[group, rows]
        one = e_flat[group, rows]
        index, lat_w = [], []
        for q, w in enumerate((1.0 - one, one)):
            near = slot - olat - q
            valid = ((slot < HALO) & (near >= HALO)) | (
                (slot >= HALO) & (slot < 2 * HALO) & (near < HALO)
            )
            lat_w.append(jnp.where(valid, w, 0.0))
            index.append(jnp.bitwise_and(lane - olat - q, LANES - 1))
        chosen, lon_w = split_lon(e_olon[group, rows], e_flon[group, rows])
        loads = [lambda near, group=group: source[group, pl.ds(near, 8)]]
        x = interpolate(loads, half, index, lat_w, chosen, lon_w, SHIFTS)[0]
        for e in range(PER):
            at = base + group * PER + e
            prime[at, rows] = prime[at, rows] + jnp.where(
                keep, roll(x, (-HALO - SLOT * e) % LANES), 0.0
            )


def solve(dims, first_field, prime, ratio, inverse, coup, dep, weight, tl, z):
    fields, levels = dims
    members = range(first_field, first_field + PAIR)
    x = {}
    for k in range(levels):
        for f in members:
            at = f * levels + k
            value = prime[at]
            if k > 0:
                value = value + coup[f * (levels - 1) + k - 1] * x[f]
            x[f] = value * inverse[at]
            prime[at] = x[f]
    for k in range(levels - 1, -1, -1):
        for f in members:
            at = f * levels + k
            x[f] = prime[at] if k == levels - 1 else prime[at] + ratio[at] * x[f]
            tl[at] = x[f]
    for k in range(levels):
        for f in members:
            at = f * levels + k
            forcing = weight[at] * (tl[at] - dep[at])
            if k > 0:
                forcing = forcing + coup[f * (levels - 1) + k - 1] * x[f]
            x[f] = forcing * inverse[at]
            prime[at] = x[f]
    for k in range(levels - 1, -1, -1):
        for f in members:
            at = f * levels + k
            x[f] = prime[at] if k == levels - 1 else prime[at] + ratio[at] * x[f]
            z[pl.ds(at * TALL + 8, 16)] = x[f]


def shifted(x, n):
    return x if n == 0 else roll(x, (-n) % LANES)


def spread_lon(dims, base, z, lonw, latw, low, high):
    @pl.loop(0, low.shape[0])
    def _(group):
        number = base + group * PER
        for out, targets, sources in (
            (low, range(-HALO, 0), range(HALO)),
            (high, range(16, 15 + HALO), range(17 - HALO, 16)),
        ):
            scaled = {}
            for j in sources:
                x = z[pick(number, 8 + j, TALL)]
                for a in targets:
                    if j - a in SHIFTS:
                        scaled[a, j] = x * lonw[SHIFTS.index(j - a), group, OUTER.index(j)]
            total = {}
            for pos, n in enumerate(SHIFTS):
                w = {j: latw[pos, group, OUTER.index(j)] for j in sources}
                for a in targets:
                    terms = [w[j] * scaled[a, j] for j in sources if (a, j) in scaled]
                    x = shifted(functools.reduce(jnp.add, terms), n)
                    total[a] = total[a] + x if a in total else x
            for e, a in enumerate(targets):
                out[group, e] = total[a]


def spread_edges(z, lonw, latw, result):
    slot = jnp.bitwise_and(lane_index((8, LANES)), SLOT - 1)

    for group in range(result.shape[0]):
        for part, steps in enumerate((range(1, HALO + 1), SHIFTS, SHIFTS, range(1 - HALO, 0))):
            sums = {}
            for r in steps:
                near = 8 * part + r
                scaled = lonw[SHIFTS.index(r), pl.ds(group * TALL + near, 8)] * z[group, pl.ds(near, 8)]
                for n in range(1, HALO + 1):
                    term = latw[n - 1, pl.ds(group * TALL + near, 8)] * scaled
                    sums[n] = sums[n] + term if n in sums else term
            total = None
            for n, x in sums.items():
                down = jnp.where((slot >= HALO - n) & (slot < HALO), shifted(x, n), 0.0)
                up = jnp.where((slot >= HALO) & (slot < HALO + n), shifted(x, -n), 0.0)
                total = down + up if total is None else total + (down + up)
            result[group, 8 * part : 8 * part + 8] = total


def add_corners(left, right, result):
    @pl.loop(0, result.shape[0])
    def _(group):
        row = lax.broadcasted_iota(jnp.int32, (8, LANES), 0)
        result[group, 8:16] = result[group, 8:16] + jnp.where(row < HALO - 1, left[group, 8:16], 0.0)
        result[group, 16:24] = result[group, 16:24] + jnp.where(row >= 8 - HALO, right[group, 16:24], 0.0)


def gather_lon(base, from_left, from_right, grad):
    @pl.loop(0, from_left.shape[0])
    def _(group):
        number = group * PER
        for side, first in ((from_right, 16 - HALO), (from_left, 0)):
            for e in range(side.shape[1]):
                at = pick(base + number, first + e, 16)
                grad[at] = grad[at] + side[group, e]


def collect(dims, base, z, lonw, latw, grad):
    levels = dims[1]

    @pl.loop(0, levels)
    def _(k):
        for half in range(2):
            sums = {}
            for lon_pos, lon_total in enumerate(SHIFTS):
                near = 8 + 8 * half + lon_total
                scale = lonw[lon_pos, pl.ds(k * TALL + near, 8)]
                scaled = [scale * z[pl.ds((base + f * levels + k) * TALL + near, 8)] for f in range(PAIR)]
                for pos in range(len(SHIFTS)):
                    w = latw[pos, pl.ds(k * TALL + near, 8)]
                    for f in range(PAIR):
                        term = w * scaled[f]
                        sums[f, pos] = term if lon_pos == 0 else sums[f, pos] + term
            for f in range(PAIR):
                at = pl.ds((base + f * levels + k) * 16 + 8 * half, 8)
                total = grad[at]
                for pos, n in enumerate(SHIFTS):
                    total = total + shifted(sums[f, pos], n)
                grad[at] = total


def finish(base, band, bands, edges, grad):
    has_lower = band > 0
    has_upper = band < bands - 1

    for group in range(edges.shape[1]):
        lower = jnp.where(has_lower, edges[0, group], 0.0)
        upper = jnp.where(has_upper, edges[1, group], 0.0)
        lane = lane_index(lower.shape)
        x = jnp.where(jnp.bitwise_and(lane, SLOT - 1) < HALO, upper, lower)
        keep = edge_mask(lane)
        for e in range(PER):
            at = tile(base + group * PER + e)
            grad[at] = grad[at] + jnp.where(keep, roll(x, (-HALO - SLOT * e) % LANES), 0.0)


def kernel(
    dims, sizes,
    inc_h, dep_h, weight_h, olon_h, olat_h, flon_h, flat_h, coup_h,
    tl, grad,
    wide, dep, weight, olon, olat, flon, flat, coup,
    edge_out, edge_in, e_source, e_olon, e_olat, e_flon, e_flat, e_lonw, e_latw, e_z,
    low, high, from_left, from_right, back_out, back_in, corner_left, corner_right,
    lonw, latw, t_lonw, t_latw, prime, ratio, inverse, z,
    load_sem, send, recv,
):
    fields, levels = dims
    pairs = fields // PAIR
    per_pair = PAIR * levels
    at = neighbours(sizes)
    band, bands = lax.axis_index("lat"), sizes[0]
    has_lower = band > 0
    has_upper = band < bands - 1
    numbers = iter(range(send.shape[0]))

    copies = [
        (olon_h, olon), (olat_h, olat), (flon_h, flon), (flat_h, flat),
        (inc_h, wide.at[:, 8:24]), (coup_h, coup), (dep_h, dep), (weight_h, weight),
    ]
    spare = olon.shape[0] - levels * 16
    for src, dst in copies[:4]:
        copies.append((src.at[0:spare], dst.at[levels * 16 : levels * 16 + spare]))
    copies[:4] = [(src, dst.at[0 : levels * 16]) for src, dst in copies[:4]]
    loads = [pltpu.make_async_copy(src, dst, load_sem.at[i]) for i, (src, dst) in enumerate(copies)]
    for load in loads:
        load.start()

    def launch(src, dst, device):
        copy = remote(src, dst, send, recv, next(numbers), device)
        copy.start()
        return copy

    def launch_lat(src, dst):
        down = remote(src, dst.at[1], send, recv, next(numbers), at(-1, 0))
        up = remote(src, dst.at[0], send, recv, next(numbers), at(1, 0))
        pl.when(has_lower)(down.start)
        pl.when(has_upper)(up.start)
        return down, up

    def finish_lat(copies):
        down, up = copies
        pl.when(has_lower)(down.wait_send)
        pl.when(has_upper)(down.wait_recv)
        pl.when(has_upper)(up.wait_send)
        pl.when(has_lower)(up.wait_recv)

    meet = greet([at(-1, 0), at(1, 0), at(0, -1), at(0, 1)])
    loads[4].wait()
    for pair in range(pairs):
        base = pair * per_pair
        pack_edges(lambda n, base=base: wide[base + n, 8:24], edge_out.at[pair])
    for load in (*loads[:4], *loads[8:]):
        load.wait()
    packed = (e_olon, e_olat, e_flon, e_flat)
    for src, dst in zip((olon, olat, flon, flat), packed):
        pack_edges(lambda n, src=src: src[pl.ds(n % levels * 16, 16)], dst)
    meet()
    edges = [launch_lat(edge_out.at[pair], edge_in.at[pair]) for pair in range(pairs)]
    around = []
    for pair in range(pairs):
        part = pl.ds(pair * per_pair, per_pair)
        around.append([
            launch(inc_h.at[part, 0 : HALO - 1], wide.at[part, 24 : 23 + HALO], at(0, -1)),
            launch(inc_h.at[part, 16 - HALO : 16], wide.at[part, 8 - HALO : 8], at(0, 1)),
        ])

    def launch_corners(src, left, right, rows):
        return [launch(src.at[:, of], dst.at[:, to], device)
                for of, dst, to, device in zip(rows[0::2], (left, right), rows[1::2], (at(0, -1), at(0, 1)))]

    store_across(levels, t_lonw, weights, olon, flon)
    store_across(levels, t_latw, lat_weights, olat, flat)

    @pl.loop(0, levels)
    def _(k):
        store_weights(lonw, k, weights(olon[tile(k)], flon[tile(k)]))
        store_weights(latw, k, lat_weights(olat[tile(k)], flat[tile(k)]))

    @pl.loop(0, e_olon.shape[0])
    def _(group):
        store_weights(e_lonw, group, weights(e_olon[group], e_flon[group]))
        store_weights(e_latw, group, edge_weights(e_olat[group], e_flat[group]))
        e_z[group] = jnp.zeros((TALL, LANES), jnp.float32)

    @pl.loop(0, fields * levels)
    def _(n):
        z[pl.ds(n * TALL, 8)] = jnp.zeros((8, LANES), jnp.float32)
        z[pl.ds(n * TALL + 24, 8)] = jnp.zeros((8, LANES), jnp.float32)
        grad[tile(n)] = wide[n, 8:24]

    inner = []
    for pair in range(pairs):
        finish_lat(edges[pair])
        source = e_source.at[pair]
        merge_edges(band, bands, edge_in.at[pair], source)
        rows = (pl.ds(8, HALO - 1), pl.ds(24, HALO - 1), pl.ds(24 - HALO, HALO), pl.ds(8 - HALO, HALO))
        inner.append(launch_corners(source, source, source, rows))

    advect(dims, range(fields), True, UNROLL, wide, olon, olat, flon, flat, prime)
    loads[5].wait()
    factor(dims, coup, ratio, inverse)
    for load in loads[6:8]:
        load.wait()

    across, outer = [], []
    for pair in range(pairs):
        base = pair * per_pair
        for copy in around[pair]:
            copy.wait()
        members = range(pair * PAIR, pair * PAIR + PAIR)
        advect(dims, members, False, 2 * UNROLL, wide, olon, olat, flon, flat, prime)
        for copy in inner[pair]:
            copy.wait()
        advect_edges(base, e_source.at[pair], packed, prime)
        solve(dims, pair * PAIR, prime, ratio, inverse, coup, dep, weight, tl, z)
        pack_edges(lambda n, base=base: z[pl.ds((base + n) * TALL + 8, 16)], e_z)
        spread_edges(e_z, e_lonw, e_latw, back_out.at[pair])
        rows = (pl.ds(8 - HALO, HALO), pl.ds(24 - HALO, HALO), pl.ds(24, HALO - 1), pl.ds(8, HALO - 1))
        outer.append(launch_corners(back_out.at[pair], corner_right.at[pair], corner_left.at[pair], rows))
        spread_lon(dims, base, z, t_lonw, t_latw, low.at[pair], high.at[pair])
        across.append([
            launch(low.at[pair], from_right.at[pair], at(0, -1)),
            launch(high.at[pair], from_left.at[pair], at(0, 1)),
        ])

    returned = []

    def pass_back(pair):
        for copy in outer[pair]:
            copy.wait()
        add_corners(corner_left.at[pair], corner_right.at[pair], back_out.at[pair])
        returned.append(launch_lat(back_out.at[pair, :, 8:24], back_in.at[pair]))

    def close(pair):
        base = pair * per_pair
        for copy in across[pair]:
            copy.wait()
        gather_lon(base, from_left.at[pair], from_right.at[pair], grad)
        finish_lat(returned[pair])
        finish(base, band, bands, back_in.at[pair], grad)

    pass_back(0)
    for pair in range(pairs):
        collect(dims, pair * per_pair, z, lonw, latw, grad)
        if pair + 1 < pairs:
            pass_back(pair + 1)
        close(pair)


def place(a, b, a_h, b_h, sem):
    moves = [pltpu.make_async_copy(a, a_h, sem.at[0]), pltpu.make_async_copy(b, b_h, sem.at[1])]
    for move in moves:
        move.start()
    for move in moves:
        move.wait()


def shards(sizes, increment, obs_dep, obs_weight, dep_lon, dep_lat, frac_lon, frac_lat, coupling):
    fields, levels, rows, cols = increment.shape
    count = fields * levels
    pairs = fields // PAIR
    groups = PAIR * levels // PER
    spare = max(g * PER % levels for g in range(groups)) + PER - levels
    dims = (fields, levels)

    def vmem(*s, dtype=jnp.float32):
        return pltpu.VMEM(s, dtype)

    def flat2(x):
        return x.reshape(-1, cols)

    def flat3(x):
        return x.reshape(-1, rows, cols)

    field = vmem(count, rows, cols)
    level = vmem((levels + spare) * rows, cols)
    index = vmem((levels + spare) * rows, cols, dtype=jnp.int32)
    edge = vmem(groups, rows, cols)
    edge_index = vmem(groups, rows, cols, dtype=jnp.int32)
    edges = vmem(pairs, groups, TALL, cols)
    sides = vmem(pairs, 2, groups, rows, cols)
    low = vmem(pairs, groups, HALO, 8, cols)
    high = vmem(pairs, groups, HALO - 1, 8, cols)
    steps = len(SHIFTS)
    main_w = vmem(steps, levels * TALL, cols)
    edge_w = vmem(steps, groups * TALL, cols)
    outer_w = vmem(steps, groups, len(OUTER), PER, cols)
    copies = pairs * 12
    tl, grad = pl.pallas_call(
        functools.partial(kernel, dims, sizes),
        out_shape=(
            jax.ShapeDtypeStruct((count, rows, cols), jnp.float32),
            jax.ShapeDtypeStruct((count * rows, cols), jnp.float32),
        ),
        in_specs=[ANY] * 8,
        out_specs=(WITHIN, WITHIN),
        scratch_shapes=[
            vmem(count, TALL, cols), field, field, index, index, level, level,
            vmem(fields * (levels - 1), rows, cols),
            vmem(pairs, groups, rows, cols), sides, edges,
            edge_index, edge_index, edge, edge, edge_w, vmem(HALO, groups * TALL, cols), vmem(groups, TALL, cols),
            low, high, high, low, edges, sides, edges, edges,
            main_w, main_w, outer_w, outer_w, field, field, field, vmem(count * TALL, cols),
            pltpu.SemaphoreType.DMA((12,)),
            pltpu.SemaphoreType.DMA((copies,)),
            pltpu.SemaphoreType.DMA((copies,)),
        ],
        compiler_params=pltpu.CompilerParams(
            collective_id=0, has_side_effects=True, vmem_limit_bytes=LIMIT
        ),
    )(
        *(pltpu.with_memory_space_constraint(x, pltpu.HBM) for x in (
            flat3(increment), flat3(obs_dep), flat3(obs_weight), flat2(dep_lon), flat2(dep_lat),
            flat2(frac_lon), flat2(frac_lat), flat3(coupling),
        ))
    )
    tl, grad = pl.pallas_call(
        place,
        out_shape=tuple(jax.ShapeDtypeStruct(x.shape, x.dtype) for x in (tl, grad)),
        in_specs=[WITHIN] * 2,
        out_specs=(ANY, ANY),
        scratch_shapes=[pltpu.SemaphoreType.DMA((2,))],
        compiler_params=pltpu.CompilerParams(vmem_limit_bytes=4 * 1024 * 1024),
    )(tl, grad)
    return tl.reshape(increment.shape), grad.reshape(increment.shape)


def solution(mesh):
    sizes = (mesh.shape["lat"], mesh.shape["lon"])
    wide = P(None, None, "lon", "lat")
    level = P(None, "lon", "lat")
    return jax.shard_map(
        functools.partial(shards, sizes),
        mesh=mesh,
        in_specs=(wide, wide, wide, level, level, level, level, wide),
        out_specs=(wide, wide),
        check_vma=False,
    )
```
